128 devices in a mesh: row: 16 (over x, z), col: 8 (over y, core).
Axes of the slice: x: 4, y: 4, z: 4, core: 2. Of those that a mesh axis runs over, the one named last changes fastest.
Arguments:
- block_values: bfloat16 [16, 8, 256, 128, 128], P('row', 'col')
- block_rows: int32 [16, 8, 256], P('row', 'col'), may hold values from -1 to 511, as said below
- block_cols: int32 [16, 8, 256], P('row', 'col'), may hold values from -1 to 511, as said below
- cost_vec: float32 [524288], P('col')
- demand: float32 [1048576], P('row')
- lower: float32 [524288], P('col'), may hold values from -1.5 to -0.2
- upper: float32 [524288], P('col'), may hold values from 0.2 to 1.5
- bound_kind: int32 [524288], P('col'), may hold values from 0 to 3
- primal_start: float32 [524288], P('col'), may hold values from -4 to 4
- dual_start: float32 [1048576], P('row'), may hold values from 0 to 1.5
Outputs:
- primal_out: float32 [524288], P('col')
- dual_out: float32 [1048576], P('row')
The draws below stay inside these ranges and needn't reach their ends.
Inputs may be any that keep to these rules, and one draw needn't show every extreme that they name: A slot's block_rows and block_cols are both -1 exactly when the slot is empty; the live slots of a device come first, a device has at least 64 of them, and in every draw some device has all 256 slots live and some device has empty slots; every block row and every block column of the whole matrix is named by some live slot; a block place may be named by several slots. `block_cols`: as for block_rows.
All inputs are finite; a program needn't handle non-finite values.
Results may differ from the reference program's by a relative error of at most 0.0073.
Values sent between devices are 32-bit elements; how exact they have to be, the bound alone decides.
A program may use at most 64 MiB of HBM per device.

```python
import math
import jax
import jax.numpy as jnp
from jax import lax

TILE = 128
ROW_TILES = 512
COL_TILES = 512
SLOTS = 256
RUIZ_PASSES = 2
ITERS = 2
ROW_GROUPS = 16
COL_GROUPS = 8
CONSTRAINTS = 1048576
VARIABLES = 524288


def pattern(key):
    folded = jax.random.fold_in(key, 11)
    key_list = jax.random.split(folded, 4)
    devices = ROW_GROUPS * COL_GROUPS
    row_cover = ROW_TILES // COL_GROUPS
    col_cover = COL_TILES // ROW_GROUPS
    fewest = max(row_cover, col_cover)
    counts = jax.random.randint(key_list[0], (devices,), fewest, SLOTS + 1)
    busiest = jax.random.randint(key_list[1], (), 0, devices)
    device_ids = jnp.arange(devices)
    counts = jnp.where(device_ids == busiest, SLOTS, counts)
    counts = jnp.where(device_ids == (busiest + 1) % devices, fewest, counts)
    slot_ids = jnp.arange(SLOTS)[None, :]
    group_row = (device_ids // COL_GROUPS)[:, None]
    group_col = (device_ids % COL_GROUPS)[:, None]
    random_rows = jax.random.randint(key_list[2], (devices, SLOTS), 0, ROW_TILES)
    random_cols = jax.random.randint(key_list[3], (devices, SLOTS), 0, COL_TILES)
    row_ids = jnp.where(slot_ids < row_cover, slot_ids * COL_GROUPS + group_col, random_rows)
    col_ids = jnp.where(slot_ids < col_cover, slot_ids * ROW_GROUPS + group_row, random_cols)
    live_slot = slot_ids < counts[:, None]
    row_ids = jnp.where(live_slot, row_ids, -1).astype(jnp.int32)
    col_ids = jnp.where(live_slot, col_ids, -1).astype(jnp.int32)
    return (row_ids.reshape(ROW_GROUPS, COL_GROUPS, SLOTS), col_ids.reshape(ROW_GROUPS, COL_GROUPS, SLOTS))


def draw_block_rows(key, part):
    return pattern(key)[0]


def draw_block_cols(key, part):
    return pattern(key)[1]


def draw_block_values(key, part):
    key_list = jax.random.split(jax.random.fold_in(key, 3), 3)
    full_shape = (ROW_GROUPS, COL_GROUPS, SLOTS, TILE, TILE)
    entries = jax.random.normal(key_list[0], full_shape, jnp.float32)
    row_factor = jnp.exp(jax.random.uniform(key_list[1], (ROW_GROUPS, COL_GROUPS, SLOTS, TILE, 1), jnp.float32) * math.log(10.0))
    col_factor = jnp.exp(jax.random.uniform(key_list[2], (ROW_GROUPS, COL_GROUPS, SLOTS, 1, TILE), jnp.float32) * math.log(10.0))
    return (entries * row_factor * col_factor * 0.3).astype(jnp.bfloat16)


def rising_vector(key, length):
    position = jnp.arange(length).astype(jnp.float32) / max(length - 1, 1)
    rising = 1.0 + 2.0 * position
    entries = jax.random.normal(key, (length,), jnp.float32)
    return entries * rising


def draw_cost_vec(key, part):
    return rising_vector(jax.random.fold_in(key, 5), VARIABLES)


def draw_demand(key, part):
    return rising_vector(jax.random.fold_in(key, 7), CONSTRAINTS)


def with_ends(result, rng, least, top_value):
    index_at = [jax.random.randint(jax.random.fold_in(rng, axis), (), 0, length) for axis, length in enumerate(result.shape)]
    widest = result.shape.index(max(result.shape))
    beside = index_at[:widest] + [(index_at[widest] + 1) % result.shape[widest]] + index_at[widest + 1:]
    return result.at[tuple(index_at)].set(least).at[tuple(beside)].set(top_value)


def shard_levels(own_key, extent, cuts, least, largest):
    loudness = 1.0
    for dim, parts in cuts:
        steps = jax.random.uniform(jax.random.fold_in(jax.random.fold_in(own_key, 6), dim), (parts,), jnp.float32, least / len(cuts), largest / len(cuts))
        loudness = loudness * jnp.repeat(jnp.exp(steps), extent[dim] // parts).reshape((-1,) + (1,) * (len(extent) - 1 - dim))
    return loudness


def gaussian(key, dims, width, limit, cuts=(), held_as=jnp.bfloat16):
    gain = shard_levels(key, dims, cuts, -0.22, 0.18) if cuts else 1.0
    array = jax.random.normal(key, dims, jnp.float32) * width * gain
    return jnp.minimum(jnp.maximum(array, -limit), limit).astype(held_as)


def setup_inputs(seed: int = 0) -> dict:
    keys = jax.random.split(jax.random.key(seed), 11)
    return {
        "block_values": draw_block_values(jax.random.fold_in(keys[10], 71), 0),
        "block_rows": draw_block_rows(jax.random.fold_in(keys[10], 71), 0),
        "block_cols": draw_block_cols(jax.random.fold_in(keys[10], 71), 0),
        "cost_vec": draw_cost_vec(jax.random.fold_in(keys[10], 71), 0),
        "demand": draw_demand(jax.random.fold_in(keys[10], 71), 0),
        "lower": jnp.clip(-1.5 + 1.3 * jax.random.uniform(keys[5], (VARIABLES,), jnp.float32) ** shard_levels(keys[5], (VARIABLES,), ((0, 8),), -0.2, 0.2), -1.5, -0.2),
        "upper": jnp.clip(0.2 + 1.3 * jax.random.uniform(keys[6], (VARIABLES,), jnp.float32) ** shard_levels(keys[6], (VARIABLES,), ((0, 8),), -0.2, 0.2), 0.2, 1.5),
        "bound_kind": with_ends(jax.random.randint(keys[7], (VARIABLES,), 0, 4), jax.random.fold_in(keys[7], 1), 0, 3).astype(jnp.int32),
        "primal_start": gaussian(keys[8], (VARIABLES,), 0.7, 4.0, ((0, 8),), jnp.float32),
        "dual_start": jnp.clip(1.5 * jax.random.uniform(keys[9], (CONSTRAINTS,), jnp.float32) ** shard_levels(keys[9], (CONSTRAINTS,), ((0, 16),), -0.2, 0.2), 0.0, 1.5),
    }


SMALL_EPS = 1e-06
STEP_SCALE = 0.3

def pick_tiles(vector, slot_ids, tile_count):
    tile_width = vector.shape[0] // tile_count
    padded = jnp.concatenate([vector.reshape(tile_count, tile_width), jnp.zeros((1, tile_width), vector.dtype)], axis=0)
    return padded[slot_ids]

def tile_peaks(block_terms, slot_ids, tile_count):
    tile_width = block_terms.shape[1]
    return jnp.zeros((tile_count + 1, tile_width), jnp.float32).at[slot_ids].max(block_terms)[:tile_count].reshape(-1)

def tile_sums(block_terms, slot_ids, tile_count):
    tile_width = block_terms.shape[1]
    return jnp.zeros((tile_count + 1, tile_width), jnp.float32).at[slot_ids].add(block_terms)[:tile_count].reshape(-1)

def project_bounds(values, low_side, high_side, bound_types):
    lifted = jnp.where((bound_types == 1) | (bound_types == 3), jnp.maximum(values, low_side), values)
    return jnp.where((bound_types == 2) | (bound_types == 3), jnp.minimum(lifted, high_side), lifted)

def slots_of(row_ids, col_ids):
    live_slot = row_ids >= 0
    return (jnp.where(live_slot, row_ids, ROW_TILES).astype(jnp.int32), jnp.where(live_slot, col_ids, COL_TILES).astype(jnp.int32))

def reference(block_values, block_rows, block_cols, cost_vec, demand, lower, upper, bound_kind, primal_start, dual_start):
    devices = ROW_GROUPS * COL_GROUPS
    flat_values = block_values.reshape(devices, SLOTS, TILE, TILE)
    flat_rows = block_rows.reshape(devices, SLOTS)
    flat_cols = block_cols.reshape(devices, SLOTS)
    group_rows = (jnp.arange(devices) // COL_GROUPS).astype(jnp.int32)
    group_cols = (jnp.arange(devices) % COL_GROUPS).astype(jnp.int32)
    device_items = (flat_values, flat_rows, flat_cols, group_rows, group_cols)
    row_scale = jnp.ones((CONSTRAINTS,), jnp.float32)
    col_scale = jnp.ones((VARIABLES,), jnp.float32)
    for pass_index in range(RUIZ_PASSES):

        def device_peaks(device_item, row_scale=row_scale, col_scale=col_scale):
            values, row_ids, col_ids, row_group, col_group = device_item
            row_slot, col_slot = slots_of(row_ids, col_ids)
            row_part = pick_tiles(row_scale.reshape(ROW_GROUPS, -1)[row_group], row_slot, ROW_TILES)
            col_part = pick_tiles(col_scale.reshape(COL_GROUPS, -1)[col_group], col_slot, COL_TILES)
            scaled = jnp.abs(values.astype(jnp.float32)) * row_part[:, :, None] * col_part[:, None, :]
            return (tile_peaks(lax.optimization_barrier(jnp.max(scaled, axis=2)), row_slot, ROW_TILES), tile_peaks(lax.optimization_barrier(jnp.max(scaled, axis=1)), col_slot, COL_TILES))
        row_parts, col_parts = lax.map(device_peaks, device_items)
        row_peak = lax.optimization_barrier(jnp.max(row_parts.reshape(ROW_GROUPS, COL_GROUPS, -1), axis=1)).reshape(-1)
        col_peak = lax.optimization_barrier(jnp.max(col_parts.reshape(ROW_GROUPS, COL_GROUPS, -1), axis=0)).reshape(-1)
        row_scale = row_scale / jnp.sqrt(row_peak + SMALL_EPS)
        col_scale = col_scale / jnp.sqrt(col_peak + SMALL_EPS)
    scaled_cost = col_scale * cost_vec
    scaled_demand = row_scale * demand
    norm_ratio = jnp.sqrt(jnp.sum(scaled_cost * scaled_cost) + SMALL_EPS) / jnp.sqrt(jnp.sum(scaled_demand * scaled_demand) + SMALL_EPS)
    primal_step = STEP_SCALE / norm_ratio
    dual_step = STEP_SCALE * norm_ratio
    primal = primal_start / col_scale
    dual_now = dual_start / row_scale
    low_side = lower / col_scale
    high_side = upper / col_scale

    def transpose_product(weights):

        def device_term(device_item):
            values, row_ids, col_ids, row_group, col_group = device_item
            row_slot, col_slot = slots_of(row_ids, col_ids)
            picked = pick_tiles(weights.reshape(ROW_GROUPS, -1)[row_group], row_slot, ROW_TILES)
            block_terms = jnp.einsum('kij,ki->kj', values.astype(jnp.float32), picked.astype(jnp.float32))
            return tile_sums(block_terms, col_slot, COL_TILES)
        partials = lax.map(device_term, device_items)
        return lax.optimization_barrier(jnp.sum(partials.reshape(ROW_GROUPS, COL_GROUPS, -1), axis=0)).reshape(-1)

    def forward_product(shifted):

        def device_term(device_item):
            values, row_ids, col_ids, row_group, col_group = device_item
            row_slot, col_slot = slots_of(row_ids, col_ids)
            picked = pick_tiles(shifted.reshape(COL_GROUPS, -1)[col_group], col_slot, COL_TILES)
            block_terms = jnp.einsum('kij,kj->ki', values.astype(jnp.float32), picked.astype(jnp.float32))
            return tile_sums(block_terms, row_slot, ROW_TILES)
        partials = lax.map(device_term, device_items)
        return lax.optimization_barrier(jnp.sum(partials.reshape(ROW_GROUPS, COL_GROUPS, -1), axis=1)).reshape(-1)
    for pass_index in range(ITERS):
        weights = (row_scale * dual_now).astype(jnp.bfloat16)
        gradient = col_scale * transpose_product(weights)
        primal_next = project_bounds(primal - primal_step * (scaled_cost - gradient), low_side, high_side, bound_kind)
        shifted = (col_scale * (2.0 * primal_next - primal)).astype(jnp.bfloat16)
        row_image = row_scale * forward_product(shifted)
        dual_now = jnp.maximum(dual_now + dual_step * (scaled_demand - row_image), 0.0)
        primal = primal_next
    return (col_scale * primal, row_scale * dual_now)
```

```python
import functools

import jax
import jax.numpy as jnp
from jax import lax
from jax.experimental import pallas as pl
from jax.experimental.pallas import tpu as pltpu
from jax.sharding import PartitionSpec as P

SMALL_EPS = 1e-06
STEP_SCALE = 0.3
LANES = 128
GROUP = 16
CHUNKS = 8
MESH = pl.DeviceIdType.MESH
F32, BF16, I32 = jnp.float32, jnp.bfloat16, jnp.int32


def iota(shape, axis):
    return lax.broadcasted_iota(I32, shape, axis)


def dot(left, right):
    return jnp.dot(left, right, preferred_element_type=F32)


def one_hot(mask):
    return jnp.where(mask, 1.0, 0.0).astype(BF16)


def select_dot(selector, values):
    high = values.astype(BF16)
    low = (values - high.astype(F32)).astype(BF16)
    width = values.shape[1]
    both = dot(selector, jnp.concatenate([high, low], axis=1))
    return both[:, :width] + both[:, width:]


def across(column, width):
    return jnp.concatenate([column] * (width // LANES), axis=1)


def build_index(ids_ref, spread, gather, order, sorted_ids, last):
    tiles, slots = spread.shape
    lane_ids = ids_ref[...]
    column = jnp.broadcast_to(lane_ids.astype(F32), (LANES, slots)).T.astype(I32)
    spread[...] = one_hot(iota((tiles, slots), 0) == lane_ids)
    gather[...] = one_hot(iota((slots, tiles), 1) == across(column, tiles))
    wide = across(column, slots)
    down, right = iota((slots, slots), 0), iota((slots, slots), 1)
    before = (wide < lane_ids) | ((wide == lane_ids) & (down < right))
    rank = jnp.sum(jnp.where(before, 1.0, 0.0), axis=0, keepdims=True).astype(I32)
    sorter = one_hot(down == rank)
    order[...] = sorter
    coarse = (column >> 4) << 4
    parts = jnp.concatenate([coarse, column - coarse], axis=1).astype(F32).astype(BF16)
    both = dot(sorter, parts)
    in_order = both[:, :LANES] + both[:, LANES:]
    sorted_ids[...] = in_order
    following = pltpu.roll(in_order, slots - 1, 0)
    ends = (following != in_order) | (iota((slots, LANES), 0) == slots - 1)
    keys = jnp.where(ends, in_order, -5.0).T[0:1].astype(I32)
    last[...] = one_hot(iota((tiles, slots), 0) == keys)


def tile_peaks(terms, order, sorted_ids, last, exact):
    slots = terms.shape[0]
    pick = (lambda s, x: dot(s, x.astype(BF16))) if exact else select_dot
    run = pick(order[...], terms)
    ids = sorted_ids[...]
    shift = 1
    while shift < slots:
        same = pltpu.roll(ids, shift, 0) == ids
        run = jnp.maximum(run, jnp.where(same, pltpu.roll(run, shift, 0), 0.0))
        shift *= 2
    return pick(last[...], run)


def kernel(
    n_row, n_col,
    values, rows, cols, cost, demand, lower, upper, kind, primal_start, dual_start,
    primal_out, dual_out,
    kv, row_ids, col_ids, dual_full,
    cost_s, lower_s, upper_s, kind_s, primal_s, demand_s, dual_s,
    spread_r, gather_r, order_r, sorted_r, last_r,
    spread_c, gather_c, order_c, sorted_c, last_c,
    term_a, term_b, pick_a, pick_b, pick_h,
    part_r1, part_c1, part_g1, part_r2, part_c2, part_3, part_4, part_5,
    recv_r1, recv_c1, recv_g1, recv_r2, recv_c2, recv_3, recv_4, recv_5,
    full_r1, full_c1, full_2, full_3, full_4, own_primal, own_dual,
    norm_own, norm_mid, norm_x1, norm_x2,
    local_sem, chunk_sem, send_sem, recv_sem,
):
    p, q = lax.axis_index("row"), lax.axis_index("col")
    slots = kv.shape[0]
    row_tiles, col_tiles = dual_full.shape[0], part_c1.shape[0]
    row_sh, col_sh = row_tiles // n_col, col_tiles // n_row
    row_at = pl.ds(pl.multiple_of(q * row_sh, 8), row_sh)
    col_at = pl.ds(pl.multiple_of(p * col_sh, 8), col_sh)
    chunk = slots // CHUNKS

    def peer(axis, d):
        if axis == "row":
            at = lax.rem(p + d, n_row)
            return at, (at, q)
        at = lax.rem(q + d, n_col)
        return at, (p, at)

    def count(axis):
        return n_row if axis == "row" else n_col

    barrier = pltpu.get_barrier_semaphore()
    for axis in ("row", "col"):
        def greet(d, carry, axis=axis):
            pl.semaphore_signal(barrier, inc=1, device_id=peer(axis, d)[1], device_id_type=MESH)
            return carry
        lax.fori_loop(1, count(axis), greet, 0)

    local = [
        (rows, row_ids), (cols, col_ids), (dual_start, dual_full),
        (cost.at[col_at], cost_s), (lower.at[col_at], lower_s), (upper.at[col_at], upper_s),
        (kind.at[col_at], kind_s), (primal_start.at[col_at], primal_s),
        (demand.at[row_at], demand_s), (dual_start.at[row_at], dual_s),
    ]
    local = [pltpu.make_async_copy(src, dst, local_sem.at[i]) for i, (src, dst) in enumerate(local)]
    local[0].start()
    local[1].start()
    loads = []
    for i in range(CHUNKS):
        part = pl.ds(i * chunk, chunk)
        loads.append(pltpu.make_async_copy(values.at[part], kv.at[part], chunk_sem.at[i]))
        loads[-1].start()
    for copy in local[2:]:
        copy.start()

    class Exchange:
        def __init__(self, number, axis, copy):
            self.number, self.axis, self.copy = number, axis, copy

        def each(self, act):
            def body(d, carry):
                at, device = peer(self.axis, d)
                src, dst = self.copy(d, at)
                act(pltpu.make_async_remote_copy(
                    src_ref=src, dst_ref=dst, send_sem=send_sem.at[self.number, d],
                    recv_sem=recv_sem.at[self.number, d], device_id=device, device_id_type=MESH))
                return carry
            lax.fori_loop(1, count(self.axis), body, 0)

        def start(self):
            self.each(lambda c: c.start())

        def wait_recv(self):
            self.each(lambda c: c.wait_recv())

        def wait_send(self):
            self.each(lambda c: c.wait_send())

    def scatter(number, axis, part, recv):
        size = recv.shape[1]
        return Exchange(number, axis, lambda d, at: (
            part.at[pl.ds(pl.multiple_of(at * size, 8), size)], recv.at[d]))

    def spread_out(number, axis, src, dst):
        return Exchange(number, axis, lambda d, at: (src, dst))

    def collect(exchange, part, at, recv, combine):
        exchange.wait_recv()
        total = part[at, :]
        for d in range(1, recv.shape[0]):
            total = combine(total, recv[d])
        return total

    eye = iota((LANES, LANES), 0) == iota((LANES, LANES), 1)

    def on_diagonal(per_row):
        return jnp.max(jnp.where(eye, per_row, 0.0), axis=0, keepdims=True)

    def products(picked, terms, transposed):
        def body(g, carry):
            base = pl.multiple_of(g * GROUP, GROUP)
            left = picked[pl.ds(base, GROUP), :]
            place = iota((GROUP, LANES), 0)
            total = jnp.zeros((GROUP, LANES), F32)
            for b in range(GROUP):
                block = kv[base + b]
                dims = (((1,), (0,)), ((), ())) if transposed else (((1,), (1,)), ((), ()))
                result = lax.dot_general(left, block, dims, preferred_element_type=F32)
                total = jnp.where(place == b, result, total)
            terms[pl.ds(base, GROUP), :] = total
            return carry
        lax.fori_loop(0, slots // GROUP, body, 0)

    local[0].wait()
    build_index(row_ids, spread_r, gather_r, order_r, sorted_r, last_r)
    local[1].wait()
    build_index(col_ids, spread_c, gather_c, order_c, sorted_c, last_c)

    eighth = 8
    def first_peaks(g, carry):
        base = pl.multiple_of(g * eighth, eighth)
        place = iota((eighth, LANES), 0)
        by_row = jnp.zeros((eighth, LANES), F32)
        by_col = jnp.zeros((eighth, LANES), F32)
        for b in range(eighth):
            size = jnp.abs(kv[base + b].astype(F32))
            by_row = jnp.where(place == b, on_diagonal(jnp.max(size, axis=1, keepdims=True)), by_row)
            by_col = jnp.where(place == b, jnp.max(size, axis=0, keepdims=True), by_col)
        term_a[pl.ds(base, eighth), :] = by_row
        term_b[pl.ds(base, eighth), :] = by_col
        return carry
    per_chunk = chunk // eighth
    for i in range(CHUNKS):
        loads[i].wait()
        lax.fori_loop(i * per_chunk, (i + 1) * per_chunk, first_peaks, 0)

    part_r1[...] = tile_peaks(term_a[...], order_r, sorted_r, last_r, True)
    pl.semaphore_wait(barrier, n_row + n_col - 2)
    send_r1 = scatter(0, "col", part_r1, recv_r1)
    send_r1.start()
    part_c1[...] = tile_peaks(term_b[...], order_c, sorted_c, last_c, True)
    send_c1 = scatter(1, "row", part_c1, recv_c1)
    send_c1.start()

    for copy in local[2:]:
        copy.wait()
    pick_h[...] = dot(gather_r[...], dual_full[...].astype(BF16)).astype(BF16)
    products(pick_h, term_a, True)
    part_g1[...] = select_dot(spread_c[...], term_a[...])

    row_scale = 1.0 / jnp.sqrt(collect(send_r1, part_r1, row_at, recv_r1, jnp.maximum) + SMALL_EPS)
    full_r1[row_at, :] = row_scale
    share_r1 = spread_out(2, "col", full_r1.at[row_at], full_r1.at[row_at])
    share_r1.start()
    col_scale = 1.0 / jnp.sqrt(collect(send_c1, part_c1, col_at, recv_c1, jnp.maximum) + SMALL_EPS)
    full_c1[col_at, :] = col_scale
    share_c1 = spread_out(3, "row", full_c1.at[col_at], full_c1.at[col_at])
    share_c1.start()
    send_g1 = scatter(4, "row", part_g1, recv_g1)
    send_g1.start()

    share_r1.wait_recv()
    pick_a[...] = select_dot(gather_r[...], full_r1[...])
    share_c1.wait_recv()
    pick_b[...] = select_dot(gather_c[...], full_c1[...])

    def second_peaks(g, carry):
        base = pl.multiple_of(g * eighth, eighth)
        place = iota((eighth, LANES), 0)
        by_row = jnp.zeros((eighth, LANES), F32)
        by_col = jnp.zeros((eighth, LANES), F32)
        row_part = pick_a[pl.ds(base, eighth), :]
        col_part = pick_b[pl.ds(base, eighth), :]
        row_down = row_part.T
        for b in range(eighth):
            size = jnp.abs(kv[base + b].astype(F32))
            across_peak = jnp.max(size * col_part[b:b + 1], axis=1, keepdims=True)
            down_peak = jnp.max(size * row_down[:, b:b + 1], axis=0, keepdims=True)
            by_row = jnp.where(place == b, on_diagonal(across_peak), by_row)
            by_col = jnp.where(place == b, down_peak, by_col)
        term_a[pl.ds(base, eighth), :] = by_row * row_part
        term_b[pl.ds(base, eighth), :] = by_col * col_part
        return carry
    lax.fori_loop(0, slots // eighth, second_peaks, 0)

    part_r2[...] = tile_peaks(term_a[...], order_r, sorted_r, last_r, False)
    send_r2 = scatter(5, "col", part_r2, recv_r2)
    send_r2.start()
    part_c2[...] = tile_peaks(term_b[...], order_c, sorted_c, last_c, False)
    send_c2 = scatter(6, "row", part_c2, recv_c2)
    send_c2.start()
    row_scale = row_scale / jnp.sqrt(collect(send_r2, part_r2, row_at, recv_r2, jnp.maximum) + SMALL_EPS)
    col_scale = col_scale / jnp.sqrt(collect(send_c2, part_c2, col_at, recv_c2, jnp.maximum) + SMALL_EPS)

    scaled_cost = col_scale * cost_s[...]
    scaled_demand = row_scale * demand_s[...]

    def squares(x):
        return jnp.sum((x * x).reshape(-1, 8, LANES), axis=0)
    norm_own[0:8, :] = squares(scaled_cost)
    norm_own[8:16, :] = squares(scaled_demand)
    norm_1 = Exchange(7, "col", lambda d, at: (norm_own, norm_x1.at[d]))
    norm_1.start()
    primal = primal_s[...] / col_scale
    dual_now = dual_s[...] / row_scale
    low_side = lower_s[...] / col_scale
    high_side = upper_s[...] / col_scale
    bound = kind_s[...]
    norm_mid[...] = collect(norm_1, norm_own, slice(None), norm_x1, jnp.add)
    norm_2 = Exchange(8, "row", lambda d, at: (norm_mid, norm_x2.at[d]))
    norm_2.start()
    gradient = col_scale * collect(send_g1, part_g1, col_at, recv_g1, jnp.add)
    norms = collect(norm_2, norm_mid, slice(None), norm_x2, jnp.add)
    cost_total = jnp.sum(jnp.sum(norms[0:8], axis=0, keepdims=True), axis=1, keepdims=True)
    demand_total = jnp.sum(jnp.sum(norms[8:16], axis=0, keepdims=True), axis=1, keepdims=True)
    norm_ratio = jnp.sqrt(cost_total + SMALL_EPS) / jnp.sqrt(demand_total + SMALL_EPS)
    primal_step = STEP_SCALE / norm_ratio
    dual_step = STEP_SCALE * norm_ratio

    def project(x):
        x = jnp.where((bound == 1) | (bound == 3), jnp.maximum(x, low_side), x)
        return jnp.where((bound == 2) | (bound == 3), jnp.minimum(x, high_side), x)

    def forward(number, full, terms, part, recv):
        share = spread_out(number, "row", full.at[col_at], full.at[col_at])
        share.start()
        return share

    def image(share, number, full, part, recv):
        share.wait_recv()
        pick_h[...] = dot(gather_c[...], full[...].astype(BF16)).astype(BF16)
        products(pick_h, term_a, False)
        part[...] = select_dot(spread_r[...], term_a[...])
        send = scatter(number, "col", part, recv)
        send.start()
        return send

    primal_next = project(primal - primal_step * (scaled_cost - gradient))
    full_2[col_at, :] = col_scale * (2.0 * primal_next - primal)
    primal = primal_next
    share_2 = spread_out(9, "row", full_2.at[col_at], full_2.at[col_at])
    share_2.start()
    send_3 = image(share_2, 10, full_2, part_3, recv_3)
    row_image = row_scale * collect(send_3, part_3, row_at, recv_3, jnp.add)
    dual_now = jnp.maximum(dual_now + dual_step * (scaled_demand - row_image), 0.0)

    full_3[row_at, :] = row_scale * dual_now
    share_3 = spread_out(11, "col", full_3.at[row_at], full_3.at[row_at])
    share_3.start()
    share_3.wait_recv()
    pick_h[...] = dot(gather_r[...], full_3[...].astype(BF16)).astype(BF16)
    products(pick_h, term_a, True)
    part_4[...] = select_dot(spread_c[...], term_a[...])
    send_4 = scatter(12, "row", part_4, recv_4)
    send_4.start()
    gradient = col_scale * collect(send_4, part_4, col_at, recv_4, jnp.add)
    primal_next = project(primal - primal_step * (scaled_cost - gradient))
    full_4[col_at, :] = col_scale * (2.0 * primal_next - primal)
    share_4 = spread_out(13, "row", full_4.at[col_at], full_4.at[col_at])
    share_4.start()
    own_primal[...] = col_scale * primal_next
    share_p = spread_out(14, "row", own_primal, primal_out.at[col_at])
    share_p.start()
    keep_p = pltpu.make_async_copy(own_primal, primal_out.at[col_at], local_sem.at[0])
    keep_p.start()
    send_5 = image(share_4, 15, full_4, part_5, recv_5)
    row_image = row_scale * collect(send_5, part_5, row_at, recv_5, jnp.add)
    dual_now = jnp.maximum(dual_now + dual_step * (scaled_demand - row_image), 0.0)
    own_dual[...] = row_scale * dual_now
    share_d = spread_out(16, "col", own_dual, dual_out.at[row_at])
    share_d.start()
    keep_d = pltpu.make_async_copy(own_dual, dual_out.at[row_at], local_sem.at[1])
    keep_d.start()

    for exchange in (
        send_r1, send_c1, share_r1, share_c1, send_g1, send_r2, send_c2, norm_1, norm_2,
        share_2, send_3, share_3, send_4, share_4, share_p, send_5,
    ):
        exchange.wait_send()
    share_p.wait_recv()
    keep_p.wait()
    keep_d.wait()
    share_d.wait_recv()
    share_d.wait_send()


def per_device(n_row, n_col, *args):
    values, rows, cols = args[0][0, 0], args[1][0], args[2][0]
    vectors = [a.reshape(-1, LANES) for a in args[3:]]
    slots = values.shape[0]
    col_tiles, row_tiles = vectors[0].shape[0], vectors[1].shape[0]
    row_sh, col_sh = row_tiles // n_col, col_tiles // n_row
    vmem = pltpu.VMEM

    def index_scratch(tiles):
        return [
            vmem((tiles, slots), BF16), vmem((slots, tiles), BF16), vmem((slots, slots), BF16),
            vmem((slots, LANES), F32), vmem((tiles, slots), BF16),
        ]

    row_full, col_full = vmem((row_tiles, LANES), F32), vmem((col_tiles, LANES), F32)
    row_own, col_own = vmem((row_sh, LANES), F32), vmem((col_sh, LANES), F32)
    row_recv, col_recv = vmem((n_col, row_sh, LANES), F32), vmem((n_row, col_sh, LANES), F32)
    term = vmem((slots, LANES), F32)
    most = max(n_row, n_col)
    scratch = [
        vmem(values.shape, BF16), vmem((1, slots), I32), vmem((1, slots), I32), row_full,
        col_own, col_own, col_own, vmem((col_sh, LANES), I32), col_own, row_own, row_own,
        *index_scratch(row_tiles), *index_scratch(col_tiles),
        term, term, term, term, vmem((slots, LANES), BF16),
        row_full, col_full, col_full, row_full, col_full, row_full, col_full, row_full,
        row_recv, col_recv, col_recv, row_recv, col_recv, row_recv, col_recv, row_recv,
        row_full, col_full, col_full, row_full, col_full, col_own, row_own,
        vmem((16, LANES), F32), vmem((16, LANES), F32),
        vmem((n_col, 16, LANES), F32), vmem((n_row, 16, LANES), F32),
        pltpu.SemaphoreType.DMA((10,)), pltpu.SemaphoreType.DMA((CHUNKS,)),
        pltpu.SemaphoreType.DMA((17, most)), pltpu.SemaphoreType.DMA((17, most)),
    ]
    anywhere = pl.BlockSpec(memory_space=pl.ANY)
    primal, dual = pl.pallas_call(
        functools.partial(kernel, n_row, n_col),
        out_shape=(
            jax.ShapeDtypeStruct((col_tiles, LANES), F32),
            jax.ShapeDtypeStruct((row_tiles, LANES), F32),
        ),
        in_specs=[anywhere] * 10,
        out_specs=(anywhere, anywhere),
        scratch_shapes=scratch,
        compiler_params=pltpu.CompilerParams(
            collective_id=0, has_side_effects=True, vmem_limit_bytes=48 * 1024 * 1024
        ),
    )(values, rows, cols, *vectors)
    return primal.reshape(-1), dual.reshape(-1)


def solution(mesh):
    grid = P("row", "col", None)
    return jax.shard_map(
        functools.partial(per_device, mesh.shape["row"], mesh.shape["col"]),
        mesh=mesh,
        in_specs=(
            P("row", "col", None, None, None), grid, grid,
            P("col"), P("row"), P("col"), P("col"), P("col"), P("col"), P("row"),
        ),
        out_specs=(P("col"), P("row")),
        check_vma=False,
    )
```

```python
import functools

import jax
import jax.numpy as jnp
from jax import lax
from jax.experimental import pallas as pl
from jax.experimental.pallas import tpu as pltpu
from jax.sharding import PartitionSpec as P

SMALL_EPS = 1e-06
STEP_SCALE = 0.3
LANES = 128
GROUP = 16
CHUNKS = 8
MESH = pl.DeviceIdType.MESH
F32, BF16, I32 = jnp.float32, jnp.bfloat16, jnp.int32


def iota(shape, axis):
    return lax.broadcasted_iota(I32, shape, axis)


def dot(left, right):
    return jnp.dot(left, right, preferred_element_type=F32)


def one_hot(mask):
    return jnp.where(mask, 1.0, 0.0).astype(BF16)


def select_dot(selector, values):
    high = values.astype(BF16)
    low = (values - high.astype(F32)).astype(BF16)
    width = values.shape[1]
    both = dot(selector, jnp.concatenate([high, low], axis=1))
    return both[:, :width] + both[:, width:]


def across(column, width):
    return jnp.concatenate([column] * (width // LANES), axis=1)


def build_index(ids_ref, spread, gather, order, sorted_ids, last):
    tiles, slots = spread.shape
    lane_ids = ids_ref[...]
    column = jnp.broadcast_to(lane_ids.astype(F32), (LANES, slots)).T.astype(I32)
    spread[...] = one_hot(iota((tiles, slots), 0) == lane_ids)
    gather[...] = one_hot(iota((slots, tiles), 1) == across(column, tiles))
    wide = across(column, slots)
    down, right = iota((slots, slots), 0), iota((slots, slots), 1)
    before = (wide < lane_ids) | ((wide == lane_ids) & (down < right))
    rank = jnp.sum(jnp.where(before, 1.0, 0.0), axis=0, keepdims=True).astype(I32)
    sorter = one_hot(down == rank)
    order[...] = sorter
    coarse = (column >> 4) << 4
    parts = jnp.concatenate([coarse, column - coarse], axis=1).astype(F32).astype(BF16)
    both = dot(sorter, parts)
    in_order = both[:, :LANES] + both[:, LANES:]
    sorted_ids[...] = in_order
    following = pltpu.roll(in_order, slots - 1, 0)
    ends = (following != in_order) | (iota((slots, LANES), 0) == slots - 1)
    keys = jnp.where(ends, in_order, -5.0).T[0:1].astype(I32)
    last[...] = one_hot(iota((tiles, slots), 0) == keys)


def tile_peaks(terms, order, sorted_ids, last, exact):
    slots = terms.shape[0]
    pick = (lambda s, x: dot(s, x.astype(BF16))) if exact else select_dot
    run = pick(order[...], terms)
    ids = sorted_ids[...]
    shift = 1
    while shift < slots:
        same = pltpu.roll(ids, shift, 0) == ids
        run = jnp.maximum(run, jnp.where(same, pltpu.roll(run, shift, 0), 0.0))
        shift *= 2
    return pick(last[...], run)


def kernel(
    n_row, n_col,
    values, rows, cols, cost, demand, lower, upper, kind, primal_start, dual_start,
    primal_out, dual_out,
    kv, kvt, row_ids, col_ids, dual_full,
    cost_f, lower_f, upper_f, kind_f, primal_f, slope_f, demand_s, dual_s,
    spread_r, gather_r, order_r, sorted_r, last_r,
    spread_c, gather_c, order_c, sorted_c, last_c,
    term_a, term_b, pick_a, pick_b, pick_h,
    part_r1, part_c1, part_g1, part_r2, part_c2, part_3, part_4, part_5,
    recv_r1, recv_c1, recv_g1, recv_r2, recv_c2, recv_3, recv_4, recv_5,
    full_r1, full_c1, full_c2, full_g1, full_2, full_3, full_4, own_primal, own_dual,
    norm_own, norm_mid, norm_x1, norm_x2,
    local_sem, chunk_sem, send_sem, recv_sem,
):
    p, q = lax.axis_index("row"), lax.axis_index("col")
    slots = kv.shape[0]
    row_tiles, col_tiles = dual_full.shape[0], part_c1.shape[0]
    row_sh, col_sh = row_tiles // n_col, col_tiles // n_row
    row_at = pl.ds(pl.multiple_of(q * row_sh, 8), row_sh)
    col_at = pl.ds(pl.multiple_of(p * col_sh, 8), col_sh)
    chunk = slots // CHUNKS

    def ring(axis):
        count = n_row if axis == "row" else n_col
        return (count // 4, 4) if axis == "row" and count >= 16 else (count // 2, 2)

    def peer(axis, d):
        first, second = ring(axis)
        own = p if axis == "row" else q
        at = lax.rem(own // second + d // second, first) * second + lax.rem(own % second + d % second, second)
        return at, ((at, q) if axis == "row" else (p, at))

    def farthest_first(axis):
        first, second = ring(axis)
        def hops(d):
            one, two = d // second, d % second
            return min(one, first - one) + (min(two, second - two) if axis == "row" else 0)
        return sorted(range(1, first * second), key=hops, reverse=True)

    def count(axis):
        return n_row if axis == "row" else n_col

    barrier = pltpu.get_barrier_semaphore()
    for axis in ("row", "col"):
        def greet(d, carry, axis=axis):
            pl.semaphore_signal(barrier, inc=1, device_id=peer(axis, d)[1], device_id_type=MESH)
            return carry
        lax.fori_loop(1, count(axis), greet, 0)

    local = [
        (rows, row_ids), (cols, col_ids), (dual_start, dual_full),
        (cost, cost_f), (lower, lower_f), (upper, upper_f), (kind, kind_f), (primal_start, primal_f),
        (demand.at[row_at], demand_s), (dual_start.at[row_at], dual_s),
    ]
    local = [pltpu.make_async_copy(src, dst, local_sem.at[i]) for i, (src, dst) in enumerate(local)]
    local[0].start()
    local[1].start()
    loads = []
    for i in range(CHUNKS):
        part = pl.ds(i * chunk, chunk)
        loads.append(pltpu.make_async_copy(values.at[part], kv.at[part], chunk_sem.at[i]))
        loads[-1].start()
    for copy in local[2:]:
        copy.start()

    class Exchange:
        def __init__(self, number, axis, copy):
            self.number, self.axis, self.copy = number, axis, copy

        def each(self, act, unrolled=True):
            def body(d, carry):
                at, device = peer(self.axis, d)
                src, dst = self.copy(d, at)
                act(pltpu.make_async_remote_copy(
                    src_ref=src, dst_ref=dst, send_sem=send_sem.at[self.number, d],
                    recv_sem=recv_sem.at[self.number, d], device_id=device, device_id_type=MESH))
                return carry
            if unrolled:
                for d in farthest_first(self.axis):
                    body(d, 0)
            else:
                lax.fori_loop(1, count(self.axis), body, 0)

        def start(self):
            self.each(lambda c: c.start())

        def wait_recv(self):
            self.each(lambda c: c.wait_recv())

        def wait_send(self):
            self.each(lambda c: c.wait_send(), False)

    def scatter(number, axis, part, recv):
        size = recv.shape[1]
        return Exchange(number, axis, lambda d, at: (
            part.at[pl.ds(pl.multiple_of(at * size, 8), size)], recv.at[d]))

    def spread_out(number, axis, src, dst):
        return Exchange(number, axis, lambda d, at: (src, dst))

    def collect(exchange, part, at, recv, combine):
        exchange.wait_recv()
        total = part[at, :]
        for d in range(1, recv.shape[0]):
            total = combine(total, recv[d])
        return total

    def down_max(block):
        folded = jnp.max(block.reshape(-1, 16, LANES), axis=0)
        return jnp.max(folded.astype(F32), axis=0, keepdims=True)

    eye = iota((LANES, LANES), 0) == iota((LANES, LANES), 1)

    def on_diagonal(per_row):
        return jnp.max(jnp.where(eye, per_row, 0.0), axis=0, keepdims=True)

    def products(picked, terms, blocks):
        def body(g, carry):
            base = pl.multiple_of(g * GROUP, GROUP)
            left = picked[pl.ds(base, GROUP), :]
            place = iota((GROUP, LANES), 0)
            even = place % 2 == 0
            left = left.astype(F32)
            left = jnp.concatenate([jnp.where(even, left, 0.0), jnp.where(even, 0.0, left)], axis=1).astype(BF16)
            total = jnp.zeros((GROUP, LANES), F32)
            for b in range(0, GROUP, 4):
                pair = [blocks[pl.ds(base + b + i, 2)].reshape(2 * LANES, LANES) for i in (0, 2)]
                result = dot(left, jnp.concatenate(pair, axis=1))
                total = jnp.where(place // 2 == b // 2, result[:, :LANES], total)
                total = jnp.where(place // 2 == b // 2 + 1, result[:, LANES:], total)
            terms[pl.ds(base, GROUP), :] = total
            return carry
        lax.fori_loop(0, slots // GROUP, body, 0, unroll=slots // GROUP)

    local[0].wait()
    build_index(row_ids, spread_r, gather_r, order_r, sorted_r, last_r)
    local[1].wait()
    build_index(col_ids, spread_c, gather_c, order_c, sorted_c, last_c)

    eighth = 8
    def first_peaks(g, carry):
        base = pl.multiple_of(g * eighth, eighth)
        place = iota((eighth, LANES), 0)
        by_row = jnp.zeros((eighth, LANES), F32)
        by_col = jnp.zeros((eighth, LANES), F32)
        for b in range(eighth):
            block = kv[base + b]
            turned = block.T
            kvt[base + b] = turned
            by_row = jnp.where(place == b, down_max(jnp.abs(turned)), by_row)
            by_col = jnp.where(place == b, down_max(jnp.abs(block)), by_col)
        term_a[pl.ds(base, eighth), :] = by_row
        term_b[pl.ds(base, eighth), :] = by_col
        return carry
    per_chunk = chunk // eighth
    for i in range(CHUNKS):
        loads[i].wait()
        lax.fori_loop(i * per_chunk, (i + 1) * per_chunk, first_peaks, 0)

    part_c1[...] = tile_peaks(term_b[...], order_c, sorted_c, last_c, True)
    pl.semaphore_wait(barrier, n_row + n_col - 2)
    send_c1 = scatter(1, "row", part_c1, recv_c1)
    send_c1.start()
    part_r1[...] = tile_peaks(term_a[...], order_r, sorted_r, last_r, True)
    send_r1 = scatter(0, "col", part_r1, recv_r1)
    send_r1.start()

    for copy in local[2:]:
        copy.wait()
    pick_h[...] = dot(gather_r[...], dual_full[...].astype(BF16)).astype(BF16)
    products(pick_h, term_a, kv)
    part_g1[...] = select_dot(spread_c[...], term_a[...])

    row_scale = 1.0 / jnp.sqrt(collect(send_r1, part_r1, row_at, recv_r1, jnp.maximum) + SMALL_EPS)
    full_r1[row_at, :] = row_scale
    share_r1 = spread_out(2, "col", full_r1.at[row_at], full_r1.at[row_at])
    share_r1.start()
    col_scale = 1.0 / jnp.sqrt(collect(send_c1, part_c1, col_at, recv_c1, jnp.maximum) + SMALL_EPS)
    full_c1[col_at, :] = col_scale
    share_c1 = spread_out(3, "row", full_c1.at[col_at], full_c1.at[col_at])
    share_c1.start()
    send_g1 = scatter(4, "row", part_g1, recv_g1)
    send_g1.start()

    share_r1.wait_recv()
    pick_a[...] = select_dot(gather_r[...], full_r1[...])
    share_c1.wait_recv()
    pick_b[...] = select_dot(gather_c[...], full_c1[...])

    wide_at = (2 * eighth, eighth * LANES)
    spreader = one_hot(iota(wide_at, 0) % eighth == iota(wide_at, 1) // LANES)

    def second_peaks(g, carry):
        base = pl.multiple_of(g * eighth, eighth)
        place = iota((eighth, LANES), 0)
        by_row = jnp.zeros((eighth, LANES), F32)
        by_col = jnp.zeros((eighth, LANES), F32)
        row_part = pick_a[pl.ds(base, eighth), :]
        col_part = pick_b[pl.ds(base, eighth), :]
        high = row_part.astype(BF16).astype(F32)
        row_down = jnp.concatenate([high, row_part - high], axis=0).T.astype(BF16)
        for b in range(eighth):
            size = jnp.abs(kv[base + b].astype(F32)) * col_part[b:b + 1]
            across_peak = on_diagonal(jnp.max(size, axis=1, keepdims=True))
            if b % 2 == 0:
                wide = dot(row_down, spreader[:, b * LANES:(b + 2) * LANES])
            size = jnp.abs(kv[base + b].astype(F32)) * wide[:, (b % 2) * LANES:(b % 2 + 1) * LANES]
            down_peak = jnp.max(size, axis=0, keepdims=True)
            by_row = jnp.where(place == b, across_peak, by_row)
            by_col = jnp.where(place == b, down_peak, by_col)
        term_a[pl.ds(base, eighth), :] = by_row * row_part
        term_b[pl.ds(base, eighth), :] = by_col * col_part
        return carry
    half = slots // eighth // 2
    lax.fori_loop(0, half, second_peaks, 0, unroll=2)
    full_g1[col_at, :] = collect(send_g1, part_g1, col_at, recv_g1, jnp.add)
    share_g1 = spread_out(9, "row", full_g1.at[col_at], full_g1.at[col_at])
    share_g1.start()
    lax.fori_loop(half, 2 * half, second_peaks, 0, unroll=2)

    part_c2[...] = tile_peaks(term_b[...], order_c, sorted_c, last_c, False)
    send_c2 = scatter(6, "row", part_c2, recv_c2)
    send_c2.start()
    part_r2[...] = tile_peaks(term_a[...], order_r, sorted_r, last_r, False)
    send_r2 = scatter(5, "col", part_r2, recv_r2)
    send_r2.start()
    row_scale = row_scale / jnp.sqrt(collect(send_r2, part_r2, row_at, recv_r2, jnp.maximum) + SMALL_EPS)
    col_scale = col_scale / jnp.sqrt(collect(send_c2, part_c2, col_at, recv_c2, jnp.maximum) + SMALL_EPS)

    full_c2[col_at, :] = col_scale
    share_c2 = spread_out(17, "row", full_c2.at[col_at], full_c2.at[col_at])
    share_c2.start()

    scaled_cost = col_scale * cost_f[col_at, :]
    scaled_demand = row_scale * demand_s[...]

    def squares(x):
        return jnp.sum((x * x).reshape(-1, 8, LANES), axis=0)
    norm_own[0:8, :] = squares(scaled_cost)
    norm_own[8:16, :] = squares(scaled_demand)
    norm_1 = Exchange(7, "col", lambda d, at: (norm_own, norm_x1.at[d]))
    norm_1.start()
    dual_now = dual_s[...] / row_scale
    norm_mid[...] = collect(norm_1, norm_own, slice(None), norm_x1, jnp.add)
    norm_2 = Exchange(8, "row", lambda d, at: (norm_mid, norm_x2.at[d]))
    norm_2.start()

    share_g1.wait_recv()
    share_c2.wait_recv()
    step_rows = 64
    for i in range(0, col_tiles, step_rows):
        at = pl.ds(i, step_rows)
        scale = full_c2[at, :]
        primal_f[at, :] = primal_f[at, :] / scale
        lower_f[at, :] = lower_f[at, :] / scale
        upper_f[at, :] = upper_f[at, :] / scale
        slope_f[at, :] = scale * cost_f[at, :] - scale * full_g1[at, :]
    norms = collect(norm_2, norm_mid, slice(None), norm_x2, jnp.add)
    cost_total = jnp.sum(jnp.sum(norms[0:8], axis=0, keepdims=True), axis=1, keepdims=True)
    demand_total = jnp.sum(jnp.sum(norms[8:16], axis=0, keepdims=True), axis=1, keepdims=True)
    norm_ratio = jnp.sqrt(cost_total + SMALL_EPS) / jnp.sqrt(demand_total + SMALL_EPS)
    primal_step = STEP_SCALE / norm_ratio
    dual_step = STEP_SCALE * norm_ratio

    def project(x, at):
        bound = kind_f[at, :]
        x = jnp.where((bound == 1) | (bound == 3), jnp.maximum(x, lower_f[at, :]), x)
        return jnp.where((bound == 2) | (bound == 3), jnp.minimum(x, upper_f[at, :]), x)

    for i in range(0, col_tiles, step_rows):
        at = pl.ds(i, step_rows)
        primal = primal_f[at, :]
        primal_next = project(primal - primal_step * slope_f[at, :], at)
        full_2[at, :] = (full_c2[at, :] * (2.0 * primal_next - primal)).astype(BF16)
        primal_f[at, :] = primal_next

    def image(number, shifted, part, recv):
        pick_h[...] = dot(gather_c[...], shifted).astype(BF16)
        products(pick_h, term_a, kvt)
        part[...] = select_dot(spread_r[...], term_a[...])
        send = scatter(number, "col", part, recv)
        send.start()
        return send

    send_3 = image(10, full_2[...], part_3, recv_3)
    primal = primal_f[col_at, :]
    row_image = row_scale * collect(send_3, part_3, row_at, recv_3, jnp.add)
    dual_now = jnp.maximum(dual_now + dual_step * (scaled_demand - row_image), 0.0)

    full_3[row_at, :] = row_scale * dual_now
    share_3 = spread_out(11, "col", full_3.at[row_at], full_3.at[row_at])
    share_3.start()
    share_3.wait_recv()
    pick_h[...] = dot(gather_r[...], full_3[...].astype(BF16)).astype(BF16)
    products(pick_h, term_a, kv)
    part_4[...] = select_dot(spread_c[...], term_a[...])
    send_4 = scatter(12, "row", part_4, recv_4)
    send_4.start()
    gradient = col_scale * collect(send_4, part_4, col_at, recv_4, jnp.add)
    primal_next = project(primal - primal_step * (scaled_cost - gradient), col_at)
    full_4[col_at, :] = col_scale * (2.0 * primal_next - primal)
    share_4 = spread_out(13, "row", full_4.at[col_at], full_4.at[col_at])
    share_4.start()
    own_primal[...] = col_scale * primal_next
    share_p = spread_out(14, "row", own_primal, primal_out.at[col_at])
    share_p.start()
    keep_p = pltpu.make_async_copy(own_primal, primal_out.at[col_at], local_sem.at[0])
    keep_p.start()
    share_4.wait_recv()
    send_5 = image(15, full_4[...].astype(BF16), part_5, recv_5)
    row_image = row_scale * collect(send_5, part_5, row_at, recv_5, jnp.add)
    dual_now = jnp.maximum(dual_now + dual_step * (scaled_demand - row_image), 0.0)
    own_dual[...] = row_scale * dual_now
    share_d = spread_out(16, "col", own_dual, dual_out.at[row_at])
    share_d.start()
    keep_d = pltpu.make_async_copy(own_dual, dual_out.at[row_at], local_sem.at[1])
    keep_d.start()

    for exchange in (
        send_r1, send_c1, share_r1, share_c1, send_g1, send_r2, send_c2, norm_1, norm_2,
        share_g1, share_c2, send_3, share_3, send_4, share_4, share_p, send_5,
    ):
        exchange.wait_send()
    share_p.wait_recv()
    keep_p.wait()
    keep_d.wait()
    share_d.wait_recv()
    share_d.wait_send()


def per_device(n_row, n_col, *args):
    values, rows, cols = args[0][0, 0], args[1][0], args[2][0]
    vectors = [a.reshape(-1, LANES) for a in args[3:]]
    slots = values.shape[0]
    col_tiles, row_tiles = vectors[0].shape[0], vectors[1].shape[0]
    row_sh, col_sh = row_tiles // n_col, col_tiles // n_row
    vmem = pltpu.VMEM

    def index_scratch(tiles):
        return [
            vmem((tiles, slots), BF16), vmem((slots, tiles), BF16), vmem((slots, slots), BF16),
            vmem((slots, LANES), F32), vmem((tiles, slots), BF16),
        ]

    row_full, col_full = vmem((row_tiles, LANES), F32), vmem((col_tiles, LANES), F32)
    row_own, col_own = vmem((row_sh, LANES), F32), vmem((col_sh, LANES), F32)
    row_recv, col_recv = vmem((n_col, row_sh, LANES), F32), vmem((n_row, col_sh, LANES), F32)
    term = vmem((slots, LANES), F32)
    most = max(n_row, n_col)
    scratch = [
        vmem(values.shape, BF16), vmem(values.shape, BF16), vmem((1, slots), I32), vmem((1, slots), I32), row_full,
        col_full, col_full, col_full, vmem((col_tiles, LANES), I32), col_full, col_full, row_own, row_own,
        *index_scratch(row_tiles), *index_scratch(col_tiles),
        term, term, term, term, vmem((slots, LANES), BF16),
        row_full, col_full, col_full, row_full, col_full, row_full, col_full, row_full,
        row_recv, col_recv, col_recv, row_recv, col_recv, row_recv, col_recv, row_recv,
        row_full, col_full, col_full, col_full, vmem((col_tiles, LANES), BF16), row_full, col_full, col_own, row_own,
        vmem((16, LANES), F32), vmem((16, LANES), F32),
        vmem((n_col, 16, LANES), F32), vmem((n_row, 16, LANES), F32),
        pltpu.SemaphoreType.DMA((10,)), pltpu.SemaphoreType.DMA((CHUNKS,)),
        pltpu.SemaphoreType.DMA((18, most)), pltpu.SemaphoreType.DMA((18, most)),
    ]
    anywhere = pl.BlockSpec(memory_space=pltpu.HBM)
    primal, dual = pl.pallas_call(
        functools.partial(kernel, n_row, n_col),
        out_shape=(
            jax.ShapeDtypeStruct((col_tiles, LANES), F32),
            jax.ShapeDtypeStruct((row_tiles, LANES), F32),
        ),
        in_specs=[anywhere] * 10,
        out_specs=(anywhere, anywhere),
        scratch_shapes=scratch,
        compiler_params=pltpu.CompilerParams(
            collective_id=0, has_side_effects=True, vmem_limit_bytes=60 * 1024 * 1024
        ),
    )(values, rows, cols, *vectors)
    return primal.reshape(-1), dual.reshape(-1)


def solution(mesh):
    grid = P("row", "col", None)
    return jax.shard_map(
        functools.partial(per_device, mesh.shape["row"], mesh.shape["col"]),
        mesh=mesh,
        in_specs=(
            P("row", "col", None, None, None), grid, grid,
            P("col"), P("row"), P("col"), P("col"), P("col"), P("col"), P("row"),
        ),
        out_specs=(P("col"), P("row")),
        check_vma=False,
    )
```

```python
import functools

import jax
import jax.numpy as jnp
from jax import lax
from jax.experimental import pallas as pl
from jax.experimental.pallas import tpu as pltpu
from jax.sharding import PartitionSpec as P

SMALL_EPS = 1e-06
STEP_SCALE = 0.3
LANES = 128
GROUP = 16
CHUNKS = 8
MESH = pl.DeviceIdType.MESH
F32, BF16, I32 = jnp.float32, jnp.bfloat16, jnp.int32


def iota(shape, axis):
    return lax.broadcasted_iota(I32, shape, axis)


def dot(left, right):
    return jnp.dot(left, right, preferred_element_type=F32)


def one_hot(mask):
    return jnp.where(mask, 1.0, 0.0).astype(BF16)


def select_dot(selector, values):
    high = values.astype(BF16)
    low = (values - high.astype(F32)).astype(BF16)
    width = values.shape[1]
    both = dot(selector, jnp.concatenate([high, low], axis=1))
    return both[:, :width] + both[:, width:]


def across(column, width):
    return jnp.concatenate([column] * (width // LANES), axis=1)


def build_index(ids_ref, spread, gather, order, sorted_ids, last):
    tiles, slots = spread.shape
    lane_ids = ids_ref[...]
    column = jnp.broadcast_to(lane_ids.astype(F32), (LANES, slots)).T.astype(I32)
    spread[...] = one_hot(iota((tiles, slots), 0) == lane_ids)
    gather[...] = one_hot(iota((slots, tiles), 1) == across(column, tiles))
    wide = across(column, slots)
    down, right = iota((slots, slots), 0), iota((slots, slots), 1)
    before = (wide < lane_ids) | ((wide == lane_ids) & (down < right))
    rank = jnp.sum(jnp.where(before, 1.0, 0.0), axis=0, keepdims=True).astype(I32)
    sorter = one_hot(down == rank)
    order[...] = sorter
    coarse = (column >> 4) << 4
    parts = jnp.concatenate([coarse, column - coarse], axis=1).astype(F32).astype(BF16)
    both = dot(sorter, parts)
    in_order = both[:, :LANES] + both[:, LANES:]
    sorted_ids[...] = in_order
    following = pltpu.roll(in_order, slots - 1, 0)
    ends = (following != in_order) | (iota((slots, LANES), 0) == slots - 1)
    keys = jnp.where(ends, in_order, -5.0).T[0:1].astype(I32)
    last[...] = one_hot(iota((tiles, slots), 0) == keys)


def tile_peaks(terms, order, sorted_ids, last, exact):
    slots = terms.shape[0]
    pick = (lambda s, x: dot(s, x.astype(BF16))) if exact else select_dot
    run = pick(order[...], terms)
    ids = sorted_ids[...]
    shift = 1
    while shift < slots:
        same = pltpu.roll(ids, shift, 0) == ids
        run = jnp.maximum(run, jnp.where(same, pltpu.roll(run, shift, 0), 0.0))
        shift *= 2
    return pick(last[...], run)


def kernel(
    n_row, n_col,
    values, rows, cols, cost, demand, lower, upper, kind, primal_start, dual_start,
    primal_out, dual_out,
    kv, kvt, row_ids, col_ids, dual_full,
    cost_f, lower_f, upper_f, kind_f, primal_f, slope_f, demand_s, dual_s,
    spread_r, gather_r, order_r, sorted_r, last_r,
    spread_c, gather_c, order_c, sorted_c, last_c,
    term_a, term_b, pick_a, pick_b, pick_h,
    part_r1, part_c1, part_g1, part_r2, part_c2, part_3, part_4, part_5,
    recv_r1, recv_c1, recv_g1, recv_r2, recv_c2, recv_3, recv_4, recv_5,
    full_r1, full_c1, full_c2, full_g1, full_2, full_3, full_4, own_primal, own_dual,
    norm_own, norm_mid, norm_x1, norm_x2,
    local_sem, chunk_sem, send_sem, recv_sem,
):
    p, q = lax.axis_index("row"), lax.axis_index("col")
    slots = kv.shape[0]
    row_tiles, col_tiles = dual_full.shape[0], part_c1.shape[0]
    row_sh, col_sh = row_tiles // n_col, col_tiles // n_row
    row_at = pl.ds(pl.multiple_of(q * row_sh, 8), row_sh)
    col_at = pl.ds(pl.multiple_of(p * col_sh, 8), col_sh)
    chunk = slots // CHUNKS

    def ring(axis):
        count = n_row if axis == "row" else n_col
        return (count // 4, 4) if axis == "row" and count >= 16 else (count // 2, 2)

    def peer(axis, d):
        first, second = ring(axis)
        own = p if axis == "row" else q
        at = lax.rem(own // second + d // second, first) * second + lax.rem(own % second + d % second, second)
        return at, ((at, q) if axis == "row" else (p, at))

    def farthest_first(axis):
        first, second = ring(axis)
        def hops(d):
            one, two = d // second, d % second
            return min(one, first - one) + (min(two, second - two) if axis == "row" else 0)
        return sorted(range(1, first * second), key=hops, reverse=True)

    def count(axis):
        return n_row if axis == "row" else n_col

    barrier = pltpu.get_barrier_semaphore()
    for axis in ("row", "col"):
        def greet(d, carry, axis=axis):
            pl.semaphore_signal(barrier, inc=1, device_id=peer(axis, d)[1], device_id_type=MESH)
            return carry
        lax.fori_loop(1, count(axis), greet, 0)

    local = [
        (rows, row_ids), (cols, col_ids), (dual_start, dual_full),
        (cost, cost_f), (lower, lower_f), (upper, upper_f), (kind, kind_f), (primal_start, primal_f),
        (demand.at[row_at], demand_s), (dual_start.at[row_at], dual_s),
    ]
    local = [pltpu.make_async_copy(src, dst, local_sem.at[i]) for i, (src, dst) in enumerate(local)]
    local[0].start()
    local[1].start()
    loads = []
    for i in range(CHUNKS):
        part = pl.ds(i * chunk, chunk)
        loads.append(pltpu.make_async_copy(values.at[part], kv.at[part], chunk_sem.at[i]))
        loads[-1].start()
    for copy in local[2:]:
        copy.start()

    class Exchange:
        def __init__(self, number, axis, copy):
            self.number, self.axis, self.copy = number, axis, copy

        def each(self, act, unrolled=True):
            def body(d, carry):
                at, device = peer(self.axis, d)
                src, dst = self.copy(d, at)
                act(pltpu.make_async_remote_copy(
                    src_ref=src, dst_ref=dst, send_sem=send_sem.at[self.number, d],
                    recv_sem=recv_sem.at[self.number, d], device_id=device, device_id_type=MESH))
                return carry
            if unrolled:
                for d in farthest_first(self.axis):
                    body(d, 0)
            else:
                lax.fori_loop(1, count(self.axis), body, 0)

        def start(self):
            self.each(lambda c: c.start())

        def wait_recv(self):
            self.each(lambda c: c.wait_recv())

        def wait_send(self):
            self.each(lambda c: c.wait_send(), False)

    def scatter(number, axis, part, recv, piece=0, pieces=1):
        size = recv.shape[1]
        step = size // pieces
        return Exchange(number, axis, lambda d, at: (
            part.at[pl.ds(pl.multiple_of(at * size + piece * step, 8), step)],
            recv.at[d, pl.ds(piece * step, step)]))

    def spread_out(number, axis, src, dst):
        return Exchange(number, axis, lambda d, at: (src, dst))

    def collect(exchange, part, at, recv, combine):
        exchange.wait_recv()
        total = part[at, :]
        for d in range(1, recv.shape[0]):
            total = combine(total, recv[d])
        return total

    def down_max(block):
        folded = jnp.max(block.reshape(-1, 16, LANES), axis=0)
        return jnp.max(folded.astype(F32), axis=0, keepdims=True)

    eye = iota((LANES, LANES), 0) == iota((LANES, LANES), 1)

    def on_diagonal(per_row):
        chosen = jnp.zeros((8, LANES), F32)
        for i in range(0, LANES, 8):
            chosen = jnp.where(eye[i:i + 8], per_row[i:i + 8], chosen)
        return jnp.max(chosen, axis=0, keepdims=True)

    def products(picked, terms, blocks):
        def body(g, carry):
            base = pl.multiple_of(g * GROUP, GROUP)
            left = picked[pl.ds(base, GROUP), :]
            place = iota((GROUP, LANES), 0)
            even = place % 2 == 0
            left = left.astype(F32)
            left = jnp.concatenate([jnp.where(even, left, 0.0), jnp.where(even, 0.0, left)], axis=1).astype(BF16)
            total = jnp.zeros((GROUP, LANES), F32)
            for b in range(0, GROUP, 4):
                pair = [blocks[pl.ds(base + b + i, 2)].reshape(2 * LANES, LANES) for i in (0, 2)]
                result = dot(left, jnp.concatenate(pair, axis=1))
                total = jnp.where(place // 2 == b // 2, result[:, :LANES], total)
                total = jnp.where(place // 2 == b // 2 + 1, result[:, LANES:], total)
            terms[pl.ds(base, GROUP), :] = total
            return carry
        lax.fori_loop(0, slots // GROUP, body, 0, unroll=slots // GROUP)

    local[0].wait()
    build_index(row_ids, spread_r, gather_r, order_r, sorted_r, last_r)
    local[1].wait()
    build_index(col_ids, spread_c, gather_c, order_c, sorted_c, last_c)

    eighth = 8
    def first_peaks(g, carry):
        base = pl.multiple_of(g * eighth, eighth)
        place = iota((eighth, LANES), 0)
        by_row = jnp.zeros((eighth, LANES), F32)
        by_col = jnp.zeros((eighth, LANES), F32)
        for b in range(eighth):
            block = kv[base + b]
            turned = block.T
            kvt[base + b] = turned
            by_row = jnp.where(place == b, down_max(jnp.abs(turned)), by_row)
            by_col = jnp.where(place == b, down_max(jnp.abs(block)), by_col)
        term_a[pl.ds(base, eighth), :] = by_row
        term_b[pl.ds(base, eighth), :] = by_col
        return carry
    per_chunk = chunk // eighth
    for i in range(CHUNKS):
        loads[i].wait()
        lax.fori_loop(i * per_chunk, (i + 1) * per_chunk, first_peaks, 0)

    part_c1[...] = tile_peaks(term_b[...], order_c, sorted_c, last_c, True)
    pl.semaphore_wait(barrier, n_row + n_col - 2)
    send_c1 = scatter(1, "row", part_c1, recv_c1)
    send_c1.start()
    part_r1[...] = tile_peaks(term_a[...], order_r, sorted_r, last_r, True)
    send_r1 = scatter(0, "col", part_r1, recv_r1)
    send_r1.start()

    for copy in local[2:]:
        copy.wait()
    pick_h[...] = dot(gather_r[...], dual_full[...].astype(BF16)).astype(BF16)
    products(pick_h, term_a, kv)
    part_g1[...] = select_dot(spread_c[...], term_a[...])

    row_scale = 1.0 / jnp.sqrt(collect(send_r1, part_r1, row_at, recv_r1, jnp.maximum) + SMALL_EPS)
    full_r1[row_at, :] = row_scale
    share_r1 = spread_out(2, "col", full_r1.at[row_at], full_r1.at[row_at])
    share_r1.start()
    col_scale = 1.0 / jnp.sqrt(collect(send_c1, part_c1, col_at, recv_c1, jnp.maximum) + SMALL_EPS)
    full_c1[col_at, :] = col_scale
    share_c1 = spread_out(3, "row", full_c1.at[col_at], full_c1.at[col_at])
    share_c1.start()
    send_g1 = scatter(4, "row", part_g1, recv_g1)
    send_g1.start()

    share_r1.wait_recv()
    pick_a[...] = select_dot(gather_r[...], full_r1[...])
    share_c1.wait_recv()
    pick_b[...] = select_dot(gather_c[...], full_c1[...])

    wide_at = (2 * eighth, eighth * LANES)
    spreader = one_hot(iota(wide_at, 0) % eighth == iota(wide_at, 1) // LANES)

    def second_peaks(g, carry):
        base = pl.multiple_of(g * eighth, eighth)
        place = iota((eighth, LANES), 0)
        by_row = jnp.zeros((eighth, LANES), F32)
        by_col = jnp.zeros((eighth, LANES), F32)
        row_part = pick_a[pl.ds(base, eighth), :]
        col_part = pick_b[pl.ds(base, eighth), :]
        high = row_part.astype(BF16).astype(F32)
        high2 = col_part.astype(BF16).astype(F32)
        col_down = jnp.concatenate([high2, col_part - high2], axis=0).T.astype(BF16)
        row_down = jnp.concatenate([high, row_part - high], axis=0).T.astype(BF16)
        for b in range(eighth):
            if b % 4 < 2:
                if b % 2 == 0:
                    wide2 = dot(col_down, spreader[:, b * LANES:(b + 2) * LANES])
                size = jnp.abs(kvt[base + b].astype(F32)) * wide2[:, (b % 2) * LANES:(b % 2 + 1) * LANES]
                across_peak = jnp.max(size, axis=0, keepdims=True)
            else:
                size = jnp.abs(kv[base + b].astype(F32)) * col_part[b:b + 1]
                across_peak = on_diagonal(jnp.max(size, axis=1, keepdims=True))
            if b % 2 == 0:
                wide = dot(row_down, spreader[:, b * LANES:(b + 2) * LANES])
            size = jnp.abs(kv[base + b].astype(F32)) * wide[:, (b % 2) * LANES:(b % 2 + 1) * LANES]
            down_peak = jnp.max(size, axis=0, keepdims=True)
            by_row = jnp.where(place == b, across_peak, by_row)
            by_col = jnp.where(place == b, down_peak, by_col)
        term_a[pl.ds(base, eighth), :] = by_row * row_part
        term_b[pl.ds(base, eighth), :] = by_col * col_part
        return carry
    half = slots // eighth // 2
    lax.fori_loop(0, half, second_peaks, 0, unroll=4)
    full_g1[col_at, :] = collect(send_g1, part_g1, col_at, recv_g1, jnp.add)
    share_g1 = spread_out(9, "row", full_g1.at[col_at], full_g1.at[col_at])
    share_g1.start()
    lax.fori_loop(half, 2 * half, second_peaks, 0, unroll=4)

    part_c2[...] = tile_peaks(term_b[...], order_c, sorted_c, last_c, False)
    send_c2 = scatter(6, "row", part_c2, recv_c2)
    send_c2.start()
    part_r2[...] = tile_peaks(term_a[...], order_r, sorted_r, last_r, False)
    send_r2 = scatter(5, "col", part_r2, recv_r2)
    send_r2.start()
    row_scale = row_scale / jnp.sqrt(collect(send_r2, part_r2, row_at, recv_r2, jnp.maximum) + SMALL_EPS)
    col_scale = col_scale / jnp.sqrt(collect(send_c2, part_c2, col_at, recv_c2, jnp.maximum) + SMALL_EPS)

    full_c2[col_at, :] = col_scale
    share_c2 = spread_out(17, "row", full_c2.at[col_at], full_c2.at[col_at])
    share_c2.start()

    scaled_cost = col_scale * cost_f[col_at, :]
    scaled_demand = row_scale * demand_s[...]

    def squares(x):
        return jnp.sum((x * x).reshape(-1, 8, LANES), axis=0)
    norm_own[0:8, :] = squares(scaled_cost)
    norm_own[8:16, :] = squares(scaled_demand)
    norm_1 = Exchange(7, "col", lambda d, at: (norm_own, norm_x1.at[d]))
    norm_1.start()
    dual_now = dual_s[...] / row_scale
    norm_mid[...] = collect(norm_1, norm_own, slice(None), norm_x1, jnp.add)
    norm_2 = Exchange(8, "row", lambda d, at: (norm_mid, norm_x2.at[d]))
    norm_2.start()

    share_g1.wait_recv()
    share_c2.wait_recv()
    step_rows = 64
    for i in range(0, col_tiles, step_rows):
        at = pl.ds(i, step_rows)
        scale = full_c2[at, :]
        primal_f[at, :] = primal_f[at, :] / scale
        lower_f[at, :] = lower_f[at, :] / scale
        upper_f[at, :] = upper_f[at, :] / scale
        slope_f[at, :] = scale * cost_f[at, :] - scale * full_g1[at, :]
    norms = collect(norm_2, norm_mid, slice(None), norm_x2, jnp.add)
    cost_total = jnp.sum(jnp.sum(norms[0:8], axis=0, keepdims=True), axis=1, keepdims=True)
    demand_total = jnp.sum(jnp.sum(norms[8:16], axis=0, keepdims=True), axis=1, keepdims=True)
    norm_ratio = jnp.sqrt(cost_total + SMALL_EPS) / jnp.sqrt(demand_total + SMALL_EPS)
    primal_step = STEP_SCALE / norm_ratio
    dual_step = STEP_SCALE * norm_ratio

    def project(x, at):
        bound = kind_f[at, :]
        x = jnp.where((bound == 1) | (bound == 3), jnp.maximum(x, lower_f[at, :]), x)
        return jnp.where((bound == 2) | (bound == 3), jnp.minimum(x, upper_f[at, :]), x)

    for i in range(0, col_tiles, step_rows):
        at = pl.ds(i, step_rows)
        primal = primal_f[at, :]
        primal_next = project(primal - primal_step * slope_f[at, :], at)
        full_2[at, :] = (full_c2[at, :] * (2.0 * primal_next - primal)).astype(BF16)
        primal_f[at, :] = primal_next

    half_sh = row_sh // 2
    halves = [slice(h * half_sh, (h + 1) * half_sh) for h in range(2)]
    half_at = [pl.ds(pl.multiple_of(q * row_sh + h * half_sh, 8), half_sh) for h in range(2)]

    def image(numbers, shifted, part, recv):
        pick_h[...] = dot(gather_c[...], shifted).astype(BF16)
        products(pick_h, term_a, kvt)
        sends = []
        for h in range(2):
            starts = range(h * half_sh, row_tiles, row_sh)
            selector = jnp.concatenate([spread_r[i:i + half_sh, :] for i in starts], axis=0)
            sums = select_dot(selector, term_a[...])
            for j, i in enumerate(starts):
                part[i:i + half_sh, :] = sums[j * half_sh:(j + 1) * half_sh]
            sends.append(scatter(numbers[h], "col", part, recv, h, 2))
            sends[h].start()
        return sends

    def next_dual(h, send, part, recv, dual):
        send.wait_recv()
        total = part[half_at[h], :]
        for d in range(1, n_col):
            total = total + recv[d, halves[h], :]
        own = halves[h]
        return jnp.maximum(dual[own] + dual_step * (scaled_demand[own] - row_scale[own] * total), 0.0)

    send_3 = image((10, 18), full_2[...], part_3, recv_3)
    primal = primal_f[col_at, :]

    duals, share_3 = [], []
    for h in range(2):
        duals.append(next_dual(h, send_3[h], part_3, recv_3, dual_now))
        full_3[half_at[h], :] = row_scale[halves[h]] * duals[h]
        share_3.append(spread_out((11, 19)[h], "col", full_3.at[half_at[h]], full_3.at[half_at[h]]))
        share_3[h].start()
    dual_now = jnp.concatenate(duals, axis=0)
    for share in share_3:
        share.wait_recv()
    pick_h[...] = dot(gather_r[...], full_3[...].astype(BF16)).astype(BF16)
    products(pick_h, term_a, kv)
    part_4[...] = select_dot(spread_c[...], term_a[...])
    send_4 = scatter(12, "row", part_4, recv_4)
    send_4.start()
    gradient = col_scale * collect(send_4, part_4, col_at, recv_4, jnp.add)
    primal_next = project(primal - primal_step * (scaled_cost - gradient), col_at)
    full_4[col_at, :] = col_scale * (2.0 * primal_next - primal)
    share_4 = spread_out(13, "row", full_4.at[col_at], full_4.at[col_at])
    share_4.start()
    own_primal[...] = col_scale * primal_next
    share_p = spread_out(14, "row", own_primal, primal_out.at[col_at])
    share_p.start()
    keep_p = pltpu.make_async_copy(own_primal, primal_out.at[col_at], local_sem.at[0])
    keep_p.start()
    share_4.wait_recv()
    send_5 = image((15, 20), full_4[...].astype(BF16), part_5, recv_5)
    share_d, keep_d = [], []
    for h in range(2):
        own_dual[halves[h], :] = row_scale[halves[h]] * next_dual(h, send_5[h], part_5, recv_5, dual_now)
        source, target = own_dual.at[pl.ds(h * half_sh, half_sh)], dual_out.at[half_at[h]]
        share_d.append(spread_out((16, 21)[h], "col", source, target))
        share_d[h].start()
        keep_d.append(pltpu.make_async_copy(source, target, local_sem.at[1 + h]))
        keep_d[h].start()

    for exchange in (
        send_r1, send_c1, share_r1, share_c1, send_g1, share_g1, send_r2, send_c2, share_c2, norm_1, norm_2,
        *send_3, *share_3, send_4, share_4, share_p, *send_5,
    ):
        exchange.wait_send()
    share_p.wait_recv()
    keep_p.wait()
    for h in range(2):
        keep_d[h].wait()
    for share in share_d:
        share.wait_recv()
    for share in share_d:
        share.wait_send()


def keep(primal, dual, primal_out, dual_out, primal_held, dual_held, sems):
    reads, writes = [], []
    for source, held, target in ((primal, primal_held, primal_out), (dual, dual_held, dual_out)):
        half = held.shape[0] // 2
        for start in (0, half):
            at, number = pl.ds(start, half), len(reads)
            reads.append(pltpu.make_async_copy(source.at[at], held.at[at], sems.at[number]))
            writes.append(pltpu.make_async_copy(held.at[at], target.at[at], sems.at[4 + number]))
    for read in reads:
        read.start()
    for read, write in zip(reads, writes):
        read.wait()
        write.start()
    for write in writes:
        write.wait()


def per_device(n_row, n_col, *args):
    values, rows, cols = args[0][0, 0], args[1][0], args[2][0]
    vectors = [a.reshape(-1, LANES) for a in args[3:]]
    slots = values.shape[0]
    col_tiles, row_tiles = vectors[0].shape[0], vectors[1].shape[0]
    row_sh, col_sh = row_tiles // n_col, col_tiles // n_row
    vmem = pltpu.VMEM

    def index_scratch(tiles):
        return [
            vmem((tiles, slots), BF16), vmem((slots, tiles), BF16), vmem((slots, slots), BF16),
            vmem((slots, LANES), F32), vmem((tiles, slots), BF16),
        ]

    row_full, col_full = vmem((row_tiles, LANES), F32), vmem((col_tiles, LANES), F32)
    row_own, col_own = vmem((row_sh, LANES), F32), vmem((col_sh, LANES), F32)
    row_recv, col_recv = vmem((n_col, row_sh, LANES), F32), vmem((n_row, col_sh, LANES), F32)
    term = vmem((slots, LANES), F32)
    most = max(n_row, n_col)
    scratch = [
        vmem(values.shape, BF16), vmem(values.shape, BF16), vmem((1, slots), I32), vmem((1, slots), I32), row_full,
        col_full, col_full, col_full, vmem((col_tiles, LANES), I32), col_full, col_full, row_own, row_own,
        *index_scratch(row_tiles), *index_scratch(col_tiles),
        term, term, term, term, vmem((slots, LANES), BF16),
        row_full, col_full, col_full, row_full, col_full, row_full, col_full, row_full,
        row_recv, col_recv, col_recv, row_recv, col_recv, row_recv, col_recv, row_recv,
        row_full, col_full, col_full, col_full, vmem((col_tiles, LANES), BF16), row_full, col_full, col_own, row_own,
        vmem((16, LANES), F32), vmem((16, LANES), F32),
        vmem((n_col, 16, LANES), F32), vmem((n_row, 16, LANES), F32),
        pltpu.SemaphoreType.DMA((10,)), pltpu.SemaphoreType.DMA((CHUNKS,)),
        pltpu.SemaphoreType.DMA((22, most)), pltpu.SemaphoreType.DMA((22, most)),
    ]
    anywhere = pl.BlockSpec(memory_space=pltpu.HBM)
    primal, dual = pl.pallas_call(
        functools.partial(kernel, n_row, n_col),
        out_shape=(
            jax.ShapeDtypeStruct((col_tiles, LANES), F32),
            jax.ShapeDtypeStruct((row_tiles, LANES), F32),
        ),
        in_specs=[anywhere] * 10,
        out_specs=(anywhere, anywhere),
        scratch_shapes=scratch,
        compiler_params=pltpu.CompilerParams(
            collective_id=0, has_side_effects=True, vmem_limit_bytes=60 * 1024 * 1024
        ),
    )(values, rows, cols, *vectors)
    primal, dual = pl.pallas_call(
        keep,
        out_shape=(
            jax.ShapeDtypeStruct((col_tiles, LANES), F32),
            jax.ShapeDtypeStruct((row_tiles, LANES), F32),
        ),
        in_specs=[anywhere] * 2,
        out_specs=(anywhere, anywhere),
        scratch_shapes=[col_full, row_full, pltpu.SemaphoreType.DMA((8,))],
    )(primal, dual)
    return primal.reshape(-1), dual.reshape(-1)


def solution(mesh):
    grid = P("row", "col", None)
    return jax.shard_map(
        functools.partial(per_device, mesh.shape["row"], mesh.shape["col"]),
        mesh=mesh,
        in_specs=(
            P("row", "col", None, None, None), grid, grid,
            P("col"), P("row"), P("col"), P("col"), P("col"), P("col"), P("row"),
        ),
        out_specs=(P("col"), P("row")),
        check_vma=False,
    )
```

```python
import functools

import jax
import jax.numpy as jnp
from jax import lax
from jax.experimental import pallas as pl
from jax.experimental.pallas import tpu as pltpu
from jax.sharding import PartitionSpec as P

SMALL_EPS = 1e-06
STEP_SCALE = 0.3
LANES = 128
GROUP = 16
CHUNKS = 8
MESH = pl.DeviceIdType.MESH
F32, BF16, I32 = jnp.float32, jnp.bfloat16, jnp.int32


def iota(shape, axis):
    return lax.broadcasted_iota(I32, shape, axis)


def dot(left, right):
    return jnp.dot(left, right, preferred_element_type=F32)


def one_hot(mask):
    return jnp.where(mask, 1.0, 0.0).astype(BF16)


def select_dot(selector, values):
    high = values.astype(BF16)
    low = (values - high.astype(F32)).astype(BF16)
    width = values.shape[1]
    both = dot(selector, jnp.concatenate([high, low], axis=1))
    return both[:, :width] + both[:, width:]


def across(column, width):
    return jnp.concatenate([column] * (width // LANES), axis=1)


def build_index(ids_ref, spread, gather, order, sorted_ids, last):
    tiles, slots = spread.shape
    lane_ids = ids_ref[...]
    column = jnp.broadcast_to(lane_ids.astype(F32), (LANES, slots)).T.astype(I32)
    spread[...] = one_hot(iota((tiles, slots), 0) == lane_ids)
    gather[...] = one_hot(iota((slots, tiles), 1) == across(column, tiles))
    wide = across(column, slots)
    down, right = iota((slots, slots), 0), iota((slots, slots), 1)
    before = (wide < lane_ids) | ((wide == lane_ids) & (down < right))
    rank = jnp.sum(jnp.where(before, 1.0, 0.0), axis=0, keepdims=True).astype(I32)
    sorter = one_hot(down == rank)
    order[...] = sorter
    coarse = (column >> 4) << 4
    parts = jnp.concatenate([coarse, column - coarse], axis=1).astype(F32).astype(BF16)
    both = dot(sorter, parts)
    in_order = both[:, :LANES] + both[:, LANES:]
    sorted_ids[...] = in_order
    following = pltpu.roll(in_order, slots - 1, 0)
    ends = (following != in_order) | (iota((slots, LANES), 0) == slots - 1)
    keys = jnp.where(ends, in_order, -5.0).T[0:1].astype(I32)
    last[...] = one_hot(iota((tiles, slots), 0) == keys)


def tile_peaks(terms, order, sorted_ids, last, exact):
    slots = terms.shape[0]
    pick = (lambda s, x: dot(s, x.astype(BF16))) if exact else select_dot
    run = pick(order[...], terms)
    ids = sorted_ids[...]
    shift = 1
    while shift < slots:
        same = pltpu.roll(ids, shift, 0) == ids
        run = jnp.maximum(run, jnp.where(same, pltpu.roll(run, shift, 0), 0.0))
        shift *= 2
    return pick(last[...], run)


def kernel(
    n_row, n_col,
    values, rows, cols, cost, demand, lower, upper, kind, primal_start, dual_start,
    primal_out, dual_out,
    kv, kvt, row_ids, col_ids, dual_full,
    cost_f, lower_f, upper_f, kind_f, primal_f, slope_f, demand_s, dual_s,
    spread_r, gather_r, order_r, sorted_r, last_r,
    spread_c, gather_c, order_c, sorted_c, last_c,
    term_a, term_b, pick_a, pick_b, pick_h,
    part_r1, part_c1, part_g1, part_r2, part_c2, part_3, part_4, part_5,
    recv_r1, recv_c1, recv_g1, recv_r2, recv_c2, recv_3, recv_4, recv_5,
    full_r1, full_c1, full_c2, full_g1, full_2, full_3, full_4, own_primal, own_dual,
    norm_own, norm_mid, norm_x1, norm_x2,
    local_sem, chunk_sem, send_sem, recv_sem,
):
    p, q = lax.axis_index("row"), lax.axis_index("col")
    slots = kv.shape[0]
    row_tiles, col_tiles = dual_full.shape[0], part_c1.shape[0]
    row_sh, col_sh = row_tiles // n_col, col_tiles // n_row
    row_at = pl.ds(pl.multiple_of(q * row_sh, 8), row_sh)
    col_at = pl.ds(pl.multiple_of(p * col_sh, 8), col_sh)
    chunk = slots // CHUNKS

    def ring(axis):
        count = n_row if axis == "row" else n_col
        return (count // 4, 4) if axis == "row" and count >= 16 else (count // 2, 2)

    def peer(axis, d):
        first, second = ring(axis)
        own = p if axis == "row" else q
        at = lax.rem(own // second + d // second, first) * second + lax.rem(own % second + d % second, second)
        return at, ((at, q) if axis == "row" else (p, at))

    def farthest_first(axis):
        first, second = ring(axis)
        def hops(d):
            one, two = d // second, d % second
            return min(one, first - one) + (min(two, second - two) if axis == "row" else 0)
        return sorted(range(1, first * second), key=hops, reverse=True)

    def count(axis):
        return n_row if axis == "row" else n_col

    barrier = pltpu.get_barrier_semaphore()
    for axis in ("row", "col"):
        for d in farthest_first(axis):
            pl.semaphore_signal(barrier, inc=1, device_id=peer(axis, d)[1], device_id_type=MESH)

    local = [
        (rows, row_ids), (cols, col_ids), (dual_start, dual_full),
        (cost, cost_f), (lower, lower_f), (upper, upper_f), (kind, kind_f), (primal_start, primal_f),
        (demand.at[row_at], demand_s), (dual_start.at[row_at], dual_s),
    ]
    local = [pltpu.make_async_copy(src, dst, local_sem.at[i]) for i, (src, dst) in enumerate(local)]
    local[0].start()
    local[1].start()
    loads = []
    for i in range(CHUNKS):
        part = pl.ds(i * chunk, chunk)
        loads.append(pltpu.make_async_copy(values.at[part], kv.at[part], chunk_sem.at[i]))
        loads[-1].start()
    for copy in local[2:]:
        copy.start()

    class Exchange:
        def __init__(self, number, axis, copy):
            self.number, self.axis, self.copy = number, axis, copy

        def each(self, act, unrolled=True):
            def body(d, carry):
                at, device = peer(self.axis, d)
                src, dst = self.copy(d, at)
                act(pltpu.make_async_remote_copy(
                    src_ref=src, dst_ref=dst, send_sem=send_sem.at[self.number, d],
                    recv_sem=recv_sem.at[self.number, d], device_id=device, device_id_type=MESH))
                return carry
            if unrolled:
                for d in farthest_first(self.axis):
                    body(d, 0)
            else:
                lax.fori_loop(1, count(self.axis), body, 0)

        def start(self):
            self.each(lambda c: c.start())

        def wait_recv(self):
            self.each(lambda c: c.wait_recv())

        def wait_send(self):
            self.each(lambda c: c.wait_send(), False)

    def scatter(number, axis, part, recv, piece=0, pieces=1):
        size = recv.shape[1]
        step = size // pieces
        return Exchange(number, axis, lambda d, at: (
            part.at[pl.ds(pl.multiple_of(at * size + piece * step, 8), step)],
            recv.at[d, pl.ds(piece * step, step)]))

    def spread_out(number, axis, src, dst):
        return Exchange(number, axis, lambda d, at: (src, dst))

    def collect(exchange, part, at, recv, combine):
        exchange.wait_recv()
        total = part[at, :]
        for d in range(1, recv.shape[0]):
            total = combine(total, recv[d])
        return total

    def down_max(block):
        folded = jnp.max(block.reshape(-1, 16, LANES), axis=0)
        return jnp.max(folded.astype(F32), axis=0, keepdims=True)

    eye = iota((LANES, LANES), 0) == iota((LANES, LANES), 1)

    def on_diagonal(per_row):
        chosen = jnp.zeros((8, LANES), F32)
        for i in range(0, LANES, 8):
            chosen = jnp.where(eye[i:i + 8], per_row[i:i + 8], chosen)
        return jnp.max(chosen, axis=0, keepdims=True)

    def products(picked, terms, blocks):
        def body(g, carry):
            base = pl.multiple_of(g * GROUP, GROUP)
            left = picked[pl.ds(base, GROUP), :]
            place = iota((GROUP, LANES), 0)
            even = place % 2 == 0
            left = left.astype(F32)
            left = jnp.concatenate([jnp.where(even, left, 0.0), jnp.where(even, 0.0, left)], axis=1).astype(BF16)
            total = jnp.zeros((GROUP, LANES), F32)
            for b in range(0, GROUP, 4):
                pair = [blocks[pl.ds(base + b + i, 2)].reshape(2 * LANES, LANES) for i in (0, 2)]
                result = dot(left, jnp.concatenate(pair, axis=1))
                total = jnp.where(place // 2 == b // 2, result[:, :LANES], total)
                total = jnp.where(place // 2 == b // 2 + 1, result[:, LANES:], total)
            terms[pl.ds(base, GROUP), :] = total
            return carry
        lax.fori_loop(0, slots // GROUP, body, 0, unroll=slots // GROUP)

    local[0].wait()
    build_index(row_ids, spread_r, gather_r, order_r, sorted_r, last_r)
    local[1].wait()
    build_index(col_ids, spread_c, gather_c, order_c, sorted_c, last_c)

    eighth = 8
    def first_peaks(g, carry):
        base = pl.multiple_of(g * eighth, eighth)
        place = iota((eighth, LANES), 0)
        by_row = jnp.zeros((eighth, LANES), F32)
        by_col = jnp.zeros((eighth, LANES), F32)
        for b in range(eighth):
            block = kv[base + b]
            turned = block.T
            kvt[base + b] = turned
            by_row = jnp.where(place == b, down_max(jnp.abs(turned)), by_row)
            by_col = jnp.where(place == b, down_max(jnp.abs(block)), by_col)
        term_a[pl.ds(base, eighth), :] = by_row
        term_b[pl.ds(base, eighth), :] = by_col
        return carry
    per_chunk = chunk // eighth
    for i in range(CHUNKS):
        loads[i].wait()
        lax.fori_loop(i * per_chunk, (i + 1) * per_chunk, first_peaks, 0)

    part_c1[...] = tile_peaks(term_b[...], order_c, sorted_c, last_c, True)
    pl.semaphore_wait(barrier, n_row + n_col - 2)
    send_c1 = scatter(1, "row", part_c1, recv_c1)
    send_c1.start()
    part_r1[...] = tile_peaks(term_a[...], order_r, sorted_r, last_r, True)
    send_r1 = scatter(0, "col", part_r1, recv_r1)
    send_r1.start()

    for copy in local[2:]:
        copy.wait()
    pick_h[...] = dot(gather_r[...], dual_full[...].astype(BF16)).astype(BF16)
    products(pick_h, term_a, kv)
    part_g1[...] = select_dot(spread_c[...], term_a[...])

    row_scale = 1.0 / jnp.sqrt(collect(send_r1, part_r1, row_at, recv_r1, jnp.maximum) + SMALL_EPS)
    full_r1[row_at, :] = row_scale
    share_r1 = spread_out(2, "col", full_r1.at[row_at], full_r1.at[row_at])
    share_r1.start()
    col_scale = 1.0 / jnp.sqrt(collect(send_c1, part_c1, col_at, recv_c1, jnp.maximum) + SMALL_EPS)
    full_c1[col_at, :] = col_scale
    share_c1 = spread_out(3, "row", full_c1.at[col_at], full_c1.at[col_at])
    share_c1.start()

    share_r1.wait_recv()
    pick_a[...] = select_dot(gather_r[...], full_r1[...])
    share_c1.wait_recv()
    send_g1 = scatter(4, "row", part_g1, recv_g1)
    send_g1.start()
    pick_b[...] = select_dot(gather_c[...], full_c1[...])

    wide_at = (2 * eighth, eighth * LANES)
    spreader = one_hot(iota(wide_at, 0) % eighth == iota(wide_at, 1) // LANES)

    def second_peaks(g, carry):
        base = pl.multiple_of(g * eighth, eighth)
        place = iota((eighth, LANES), 0)
        by_row = jnp.zeros((eighth, LANES), F32)
        by_col = jnp.zeros((eighth, LANES), F32)
        row_part = pick_a[pl.ds(base, eighth), :]
        col_part = pick_b[pl.ds(base, eighth), :]
        high = row_part.astype(BF16).astype(F32)
        high2 = col_part.astype(BF16).astype(F32)
        col_down = jnp.concatenate([high2, col_part - high2], axis=0).T.astype(BF16)
        row_down = jnp.concatenate([high, row_part - high], axis=0).T.astype(BF16)
        for b in range(eighth):
            if b % 4 < 2:
                if b % 2 == 0:
                    wide2 = dot(col_down, spreader[:, b * LANES:(b + 2) * LANES])
                size = jnp.abs(kvt[base + b].astype(F32)) * wide2[:, (b % 2) * LANES:(b % 2 + 1) * LANES]
                across_peak = jnp.max(size, axis=0, keepdims=True)
            else:
                size = jnp.abs(kv[base + b].astype(F32)) * col_part[b:b + 1]
                across_peak = on_diagonal(jnp.max(size, axis=1, keepdims=True))
            if b % 2 == 0:
                wide = dot(row_down, spreader[:, b * LANES:(b + 2) * LANES])
            size = jnp.abs(kv[base + b].astype(F32)) * wide[:, (b % 2) * LANES:(b % 2 + 1) * LANES]
            down_peak = jnp.max(size, axis=0, keepdims=True)
            by_row = jnp.where(place == b, across_peak, by_row)
            by_col = jnp.where(place == b, down_peak, by_col)
        term_a[pl.ds(base, eighth), :] = by_row * row_part
        term_b[pl.ds(base, eighth), :] = by_col * col_part
        return carry
    most = slots // eighth // 4 * 3
    lax.fori_loop(0, most, second_peaks, 0, unroll=4)
    full_g1[col_at, :] = collect(send_g1, part_g1, col_at, recv_g1, jnp.add)
    share_g1 = spread_out(9, "row", full_g1.at[col_at], full_g1.at[col_at])
    share_g1.start()
    lax.fori_loop(most, slots // eighth, second_peaks, 0, unroll=4)

    part_c2[...] = tile_peaks(term_b[...], order_c, sorted_c, last_c, False)
    send_c2 = scatter(6, "row", part_c2, recv_c2)
    send_c2.start()
    part_r2[...] = tile_peaks(term_a[...], order_r, sorted_r, last_r, False)
    send_r2 = scatter(5, "col", part_r2, recv_r2)
    send_r2.start()
    row_scale = row_scale / jnp.sqrt(collect(send_r2, part_r2, row_at, recv_r2, jnp.maximum) + SMALL_EPS)
    col_scale = col_scale / jnp.sqrt(collect(send_c2, part_c2, col_at, recv_c2, jnp.maximum) + SMALL_EPS)

    full_c2[col_at, :] = col_scale
    share_c2 = spread_out(17, "row", full_c2.at[col_at], full_c2.at[col_at])
    share_c2.start()

    scaled_cost = col_scale * cost_f[col_at, :]
    scaled_demand = row_scale * demand_s[...]

    def squares(x):
        return jnp.sum((x * x).reshape(-1, 8, LANES), axis=0)
    norm_own[0:8, :] = squares(scaled_cost)
    norm_own[8:16, :] = squares(scaled_demand)
    norm_1 = Exchange(7, "col", lambda d, at: (norm_own, norm_x1.at[d]))
    norm_1.start()
    dual_now = dual_s[...] / row_scale
    norm_mid[...] = collect(norm_1, norm_own, slice(None), norm_x1, jnp.add)
    norm_2 = Exchange(8, "row", lambda d, at: (norm_mid, norm_x2.at[d]))
    norm_2.start()

    share_g1.wait_recv()
    share_c2.wait_recv()
    step_rows = 64
    for i in range(0, col_tiles, step_rows):
        at = pl.ds(i, step_rows)
        scale = full_c2[at, :]
        primal_f[at, :] = primal_f[at, :] / scale
        lower_f[at, :] = lower_f[at, :] / scale
        upper_f[at, :] = upper_f[at, :] / scale
        slope_f[at, :] = scale * cost_f[at, :] - scale * full_g1[at, :]
    norms = collect(norm_2, norm_mid, slice(None), norm_x2, jnp.add)
    cost_total = jnp.sum(jnp.sum(norms[0:8], axis=0, keepdims=True), axis=1, keepdims=True)
    demand_total = jnp.sum(jnp.sum(norms[8:16], axis=0, keepdims=True), axis=1, keepdims=True)
    norm_ratio = jnp.sqrt(cost_total + SMALL_EPS) / jnp.sqrt(demand_total + SMALL_EPS)
    primal_step = STEP_SCALE / norm_ratio
    dual_step = STEP_SCALE * norm_ratio

    def project(x, at):
        bound = kind_f[at, :]
        x = jnp.where((bound == 1) | (bound == 3), jnp.maximum(x, lower_f[at, :]), x)
        return jnp.where((bound == 2) | (bound == 3), jnp.minimum(x, upper_f[at, :]), x)

    for i in range(0, col_tiles, step_rows):
        at = pl.ds(i, step_rows)
        primal = primal_f[at, :]
        primal_next = project(primal - primal_step * slope_f[at, :], at)
        full_2[at, :] = (full_c2[at, :] * (2.0 * primal_next - primal)).astype(BF16)
        primal_f[at, :] = primal_next

    half_sh = row_sh // 2
    halves = [slice(h * half_sh, (h + 1) * half_sh) for h in range(2)]
    half_at = [pl.ds(pl.multiple_of(q * row_sh + h * half_sh, 8), half_sh) for h in range(2)]

    def image(numbers, shifted, part, recv):
        pick_h[...] = dot(gather_c[...], shifted).astype(BF16)
        products(pick_h, term_a, kvt)
        sends = []
        for h in range(2):
            starts = range(h * half_sh, row_tiles, row_sh)
            selector = jnp.concatenate([spread_r[i:i + half_sh, :] for i in starts], axis=0)
            sums = select_dot(selector, term_a[...])
            for j, i in enumerate(starts):
                part[i:i + half_sh, :] = sums[j * half_sh:(j + 1) * half_sh]
            sends.append(scatter(numbers[h], "col", part, recv, h, 2))
            sends[h].start()
        return sends

    def next_dual(h, send, part, recv, dual):
        send.wait_recv()
        total = part[half_at[h], :]
        for d in range(1, n_col):
            total = total + recv[d, halves[h], :]
        own = halves[h]
        return jnp.maximum(dual[own] + dual_step * (scaled_demand[own] - row_scale[own] * total), 0.0)

    send_3 = image((10, 18), full_2[...], part_3, recv_3)
    primal = primal_f[col_at, :]

    duals, share_3 = [], []
    for h in range(2):
        duals.append(next_dual(h, send_3[h], part_3, recv_3, dual_now))
        full_3[half_at[h], :] = row_scale[halves[h]] * duals[h]
        share_3.append(spread_out((11, 19)[h], "col", full_3.at[half_at[h]], full_3.at[half_at[h]]))
        share_3[h].start()
    dual_now = jnp.concatenate(duals, axis=0)
    for share in share_3:
        share.wait_recv()
    pick_h[...] = dot(gather_r[...], full_3[...].astype(BF16)).astype(BF16)
    products(pick_h, term_a, kv)
    part_4[...] = select_dot(spread_c[...], term_a[...])
    send_4 = scatter(12, "row", part_4, recv_4)
    send_4.start()
    gradient = col_scale * collect(send_4, part_4, col_at, recv_4, jnp.add)
    primal_next = project(primal - primal_step * (scaled_cost - gradient), col_at)
    full_4[col_at, :] = col_scale * (2.0 * primal_next - primal)
    share_4 = spread_out(13, "row", full_4.at[col_at], full_4.at[col_at])
    share_4.start()
    own_primal[...] = col_scale * primal_next
    keep_p = pltpu.make_async_copy(own_primal, primal_out.at[col_at], local_sem.at[0])
    keep_p.start()
    share_4.wait_recv()
    send_5 = image((15, 20), full_4[...].astype(BF16), part_5, recv_5)
    share_p = spread_out(14, "row", own_primal, primal_out.at[col_at])
    share_p.start()
    share_d, keep_d = [], []
    for h in range(2):
        own_dual[halves[h], :] = row_scale[halves[h]] * next_dual(h, send_5[h], part_5, recv_5, dual_now)
        source, target = own_dual.at[pl.ds(h * half_sh, half_sh)], dual_out.at[half_at[h]]
        share_d.append(spread_out((16, 21)[h], "col", source, target))
        share_d[h].start()
        keep_d.append(pltpu.make_async_copy(source, target, local_sem.at[1 + h]))
        keep_d[h].start()

    for exchange in (
        send_r1, send_c1, share_r1, share_c1, send_g1, share_g1, send_r2, send_c2, share_c2, norm_1, norm_2,
        *send_3, *share_3, send_4, share_4, share_p, *send_5,
    ):
        exchange.wait_send()
    share_p.wait_recv()
    keep_p.wait()
    for h in range(2):
        keep_d[h].wait()
    for share in share_d:
        share.wait_recv()
    for share in share_d:
        share.wait_send()


def keep(primal, dual, primal_out, dual_out, primal_held, dual_held, sems):
    reads, writes = [], []
    for source, held, target in ((primal, primal_held, primal_out), (dual, dual_held, dual_out)):
        half = held.shape[0] // 2
        for start in (0, half):
            at, number = pl.ds(start, half), len(reads)
            reads.append(pltpu.make_async_copy(source.at[at], held.at[at], sems.at[number]))
            writes.append(pltpu.make_async_copy(held.at[at], target.at[at], sems.at[4 + number]))
    for read in reads:
        read.start()
    for read, write in zip(reads, writes):
        read.wait()
        write.start()
    for write in writes:
        write.wait()


def per_device(n_row, n_col, *args):
    values, rows, cols = args[0][0, 0], args[1][0], args[2][0]
    vectors = [a.reshape(-1, LANES) for a in args[3:]]
    slots = values.shape[0]
    col_tiles, row_tiles = vectors[0].shape[0], vectors[1].shape[0]
    row_sh, col_sh = row_tiles // n_col, col_tiles // n_row
    vmem = pltpu.VMEM

    def index_scratch(tiles):
        return [
            vmem((tiles, slots), BF16), vmem((slots, tiles), BF16), vmem((slots, slots), BF16),
            vmem((slots, LANES), F32), vmem((tiles, slots), BF16),
        ]

    row_full, col_full = vmem((row_tiles, LANES), F32), vmem((col_tiles, LANES), F32)
    row_own, col_own = vmem((row_sh, LANES), F32), vmem((col_sh, LANES), F32)
    row_recv, col_recv = vmem((n_col, row_sh, LANES), F32), vmem((n_row, col_sh, LANES), F32)
    term = vmem((slots, LANES), F32)
    most = max(n_row, n_col)
    scratch = [
        vmem(values.shape, BF16), vmem(values.shape, BF16), vmem((1, slots), I32), vmem((1, slots), I32), row_full,
        col_full, col_full, col_full, vmem((col_tiles, LANES), I32), col_full, col_full, row_own, row_own,
        *index_scratch(row_tiles), *index_scratch(col_tiles),
        term, term, term, term, vmem((slots, LANES), BF16),
        row_full, col_full, col_full, row_full, col_full, row_full, col_full, row_full,
        row_recv, col_recv, col_recv, row_recv, col_recv, row_recv, col_recv, row_recv,
        row_full, col_full, col_full, col_full, vmem((col_tiles, LANES), BF16), row_full, col_full, col_own, row_own,
        vmem((16, LANES), F32), vmem((16, LANES), F32),
        vmem((n_col, 16, LANES), F32), vmem((n_row, 16, LANES), F32),
        pltpu.SemaphoreType.DMA((10,)), pltpu.SemaphoreType.DMA((CHUNKS,)),
        pltpu.SemaphoreType.DMA((22, most)), pltpu.SemaphoreType.DMA((22, most)),
    ]
    anywhere = pl.BlockSpec(memory_space=pltpu.HBM)
    primal, dual = pl.pallas_call(
        functools.partial(kernel, n_row, n_col),
        out_shape=(
            jax.ShapeDtypeStruct((col_tiles, LANES), F32),
            jax.ShapeDtypeStruct((row_tiles, LANES), F32),
        ),
        in_specs=[anywhere] * 10,
        out_specs=(anywhere, anywhere),
        scratch_shapes=scratch,
        compiler_params=pltpu.CompilerParams(
            collective_id=0, has_side_effects=True, vmem_limit_bytes=60 * 1024 * 1024
        ),
    )(values, rows, cols, *vectors)
    primal, dual = pl.pallas_call(
        keep,
        out_shape=(
            jax.ShapeDtypeStruct((col_tiles, LANES), F32),
            jax.ShapeDtypeStruct((row_tiles, LANES), F32),
        ),
        in_specs=[anywhere] * 2,
        out_specs=(anywhere, anywhere),
        scratch_shapes=[col_full, row_full, pltpu.SemaphoreType.DMA((8,))],
    )(primal, dual)
    return primal.reshape(-1), dual.reshape(-1)


def solution(mesh):
    grid = P("row", "col", None)
    return jax.shard_map(
        functools.partial(per_device, mesh.shape["row"], mesh.shape["col"]),
        mesh=mesh,
        in_specs=(
            P("row", "col", None, None, None), grid, grid,
            P("col"), P("row"), P("col"), P("col"), P("col"), P("col"), P("row"),
        ),
        out_specs=(P("col"), P("row")),
        check_vma=False,
    )
```

```python
import functools

import jax
import jax.numpy as jnp
from jax import lax
from jax.experimental import pallas as pl
from jax.experimental.pallas import tpu as pltpu
from jax.sharding import PartitionSpec as P

SMALL_EPS = 1e-06
STEP_SCALE = 0.3
LANES = 128
GROUP = 16
CHUNKS = 8
MESH = pl.DeviceIdType.MESH
F32, BF16, I32 = jnp.float32, jnp.bfloat16, jnp.int32


def iota(shape, axis):
    return lax.broadcasted_iota(I32, shape, axis)


def dot(left, right):
    return jnp.dot(left, right, preferred_element_type=F32)


def one_hot(mask):
    return jnp.where(mask, 1.0, 0.0).astype(BF16)


def select_dot(selector, values):
    high = values.astype(BF16)
    low = (values - high.astype(F32)).astype(BF16)
    width = values.shape[1]
    both = dot(selector, jnp.concatenate([high, low], axis=1))
    return both[:, :width] + both[:, width:]


def across(column, width):
    return jnp.concatenate([column] * (width // LANES), axis=1)


def build_index(ids_ref, spread, gather, order, sorted_ids, last):
    tiles, slots = spread.shape
    lane_ids = ids_ref[...]
    column = jnp.broadcast_to(lane_ids.astype(F32), (LANES, slots)).T.astype(I32)
    spread[...] = one_hot(iota((tiles, slots), 0) == lane_ids)
    gather[...] = one_hot(iota((slots, tiles), 1) == across(column, tiles))
    wide = across(column, slots)
    down, right = iota((slots, slots), 0), iota((slots, slots), 1)
    before = (wide < lane_ids) | ((wide == lane_ids) & (down < right))
    rank = jnp.sum(jnp.where(before, 1.0, 0.0), axis=0, keepdims=True).astype(I32)
    sorter = one_hot(down == rank)
    order[...] = sorter
    coarse = (column >> 4) << 4
    parts = jnp.concatenate([coarse, column - coarse], axis=1).astype(F32).astype(BF16)
    both = dot(sorter, parts)
    in_order = both[:, :LANES] + both[:, LANES:]
    sorted_ids[...] = in_order
    following = pltpu.roll(in_order, slots - 1, 0)
    ends = (following != in_order) | (iota((slots, LANES), 0) == slots - 1)
    keys = jnp.where(ends, in_order, -5.0).T[0:1].astype(I32)
    last[...] = one_hot(iota((tiles, slots), 0) == keys)


def tile_peaks(terms, order, sorted_ids, last, exact):
    slots = terms.shape[0]
    pick = (lambda s, x: dot(s, x.astype(BF16))) if exact else select_dot
    run = pick(order[...], terms)
    ids = sorted_ids[...]
    shift = 1
    while shift < slots:
        same = pltpu.roll(ids, shift, 0) == ids
        run = jnp.maximum(run, jnp.where(same, pltpu.roll(run, shift, 0), 0.0))
        shift *= 2
    return pick(last[...], run)


def kernel(
    n_row, n_col,
    values, rows, cols, cost, demand, lower, upper, kind, primal_start, dual_start,
    primal_out, dual_out,
    kv, kvt, row_ids, col_ids, dual_full,
    cost_f, lower_f, upper_f, kind_f, primal_f, slope_f, demand_s, dual_s,
    spread_r, gather_r, order_r, sorted_r, last_r,
    spread_c, gather_c, order_c, sorted_c, last_c,
    term_a, term_b, pick_a, pick_b, pick_h,
    part_r1, part_c1, part_g1, part_r2, part_c2, part_3, part_4, part_5,
    recv_r1, recv_c1, recv_g1, recv_r2, recv_c2, recv_3, recv_4, recv_5,
    full_r1, full_c1, full_c2, full_g1, full_2, full_3, full_4, own_primal, own_dual,
    norm_own, norm_mid, norm_x1, norm_x2,
    local_sem, chunk_sem, send_sem, recv_sem,
):
    p, q = lax.axis_index("row"), lax.axis_index("col")
    slots = kv.shape[0]
    row_tiles, col_tiles = dual_full.shape[0], part_c1.shape[0]
    row_sh, col_sh = row_tiles // n_col, col_tiles // n_row
    row_at = pl.ds(pl.multiple_of(q * row_sh, 8), row_sh)
    col_at = pl.ds(pl.multiple_of(p * col_sh, 8), col_sh)
    chunk = slots // CHUNKS

    def ring(axis):
        count = n_row if axis == "row" else n_col
        return (count // 4, 4) if axis == "row" and count >= 16 else (count // 2, 2)

    def peer(axis, d):
        first, second = ring(axis)
        own = p if axis == "row" else q
        at = lax.rem(own // second + d // second, first) * second + lax.rem(own % second + d % second, second)
        return at, ((at, q) if axis == "row" else (p, at))

    def farthest_first(axis):
        first, second = ring(axis)
        def hops(d):
            one, two = d // second, d % second
            return min(one, first - one) + (min(two, second - two) if axis == "row" else 0)
        return sorted(range(1, first * second), key=hops, reverse=True)

    def count(axis):
        return n_row if axis == "row" else n_col

    barrier = pltpu.get_barrier_semaphore()
    for axis in ("row", "col"):
        for d in farthest_first(axis):
            pl.semaphore_signal(barrier, inc=1, device_id=peer(axis, d)[1], device_id_type=MESH)

    local = [
        (rows, row_ids), (cols, col_ids), (dual_start, dual_full),
        (cost, cost_f), (lower, lower_f), (upper, upper_f), (kind, kind_f), (primal_start, primal_f),
        (demand.at[row_at], demand_s), (dual_start.at[row_at], dual_s),
    ]
    local = [pltpu.make_async_copy(src, dst, local_sem.at[i]) for i, (src, dst) in enumerate(local)]
    local[0].start()
    local[1].start()
    loads = []
    for i in range(CHUNKS):
        part = pl.ds(i * chunk, chunk)
        loads.append(pltpu.make_async_copy(values.at[part], kv.at[part], chunk_sem.at[i]))
        loads[-1].start()
    for copy in local[2:]:
        copy.start()

    class Exchange:
        def __init__(self, number, axis, copy):
            self.number, self.axis, self.copy = number, axis, copy

        def each(self, act, unrolled=True):
            def body(d, carry):
                at, device = peer(self.axis, d)
                src, dst = self.copy(d, at)
                act(pltpu.make_async_remote_copy(
                    src_ref=src, dst_ref=dst, send_sem=send_sem.at[self.number, d],
                    recv_sem=recv_sem.at[self.number, d], device_id=device, device_id_type=MESH))
                return carry
            if unrolled:
                for d in farthest_first(self.axis):
                    body(d, 0)
            else:
                lax.fori_loop(1, count(self.axis), body, 0)

        def start(self):
            self.each(lambda c: c.start())

        def wait_recv(self):
            self.each(lambda c: c.wait_recv())

        def wait_send(self):
            self.each(lambda c: c.wait_send(), False)

    def scatter(number, axis, part, recv, piece=0, pieces=1):
        size = recv.shape[1]
        step = size // pieces
        return Exchange(number, axis, lambda d, at: (
            part.at[pl.ds(pl.multiple_of(at * size + piece * step, 8), step)],
            recv.at[d, pl.ds(piece * step, step)]))

    def spread_out(number, axis, src, dst):
        return Exchange(number, axis, lambda d, at: (src, dst))

    def collect(exchange, part, at, recv, combine):
        exchange.wait_recv()
        total = part[at, :]
        for d in range(1, recv.shape[0]):
            total = combine(total, recv[d])
        return total

    def down_max(block):
        folded = jnp.max(block.reshape(-1, 16, LANES), axis=0)
        return jnp.max(folded.astype(F32), axis=0, keepdims=True)

    eye = iota((LANES, LANES), 0) == iota((LANES, LANES), 1)

    def on_diagonal(per_row):
        chosen = jnp.zeros((8, LANES), F32)
        for i in range(0, LANES, 8):
            chosen = jnp.where(eye[i:i + 8], per_row[i:i + 8], chosen)
        return jnp.max(chosen, axis=0, keepdims=True)

    def products(picked, terms, blocks):
        def body(g, carry):
            base = pl.multiple_of(g * GROUP, GROUP)
            left = picked[pl.ds(base, GROUP), :]
            place = iota((GROUP, LANES), 0)
            even = place % 2 == 0
            left = left.astype(F32)
            left = jnp.concatenate([jnp.where(even, left, 0.0), jnp.where(even, 0.0, left)], axis=1).astype(BF16)
            total = jnp.zeros((GROUP, LANES), F32)
            for b in range(0, GROUP, 4):
                pair = [blocks[pl.ds(base + b + i, 2)].reshape(2 * LANES, LANES) for i in (0, 2)]
                result = dot(left, jnp.concatenate(pair, axis=1))
                total = jnp.where(place // 2 == b // 2, result[:, :LANES], total)
                total = jnp.where(place // 2 == b // 2 + 1, result[:, LANES:], total)
            terms[pl.ds(base, GROUP), :] = total
            return carry
        lax.fori_loop(0, slots // GROUP, body, 0, unroll=slots // GROUP)

    local[0].wait()
    build_index(row_ids, spread_r, gather_r, order_r, sorted_r, last_r)
    local[1].wait()
    build_index(col_ids, spread_c, gather_c, order_c, sorted_c, last_c)

    eighth = 8
    def first_peaks(g, carry):
        base = pl.multiple_of(g * eighth, eighth)
        place = iota((eighth, LANES), 0)
        by_row = jnp.zeros((eighth, LANES), F32)
        by_col = jnp.zeros((eighth, LANES), F32)
        for b in range(eighth):
            block = kv[base + b]
            turned = block.T
            kvt[base + b] = turned
            by_row = jnp.where(place == b, down_max(jnp.abs(turned)), by_row)
            by_col = jnp.where(place == b, down_max(jnp.abs(block)), by_col)
        term_a[pl.ds(base, eighth), :] = by_row
        term_b[pl.ds(base, eighth), :] = by_col
        return carry
    per_chunk = chunk // eighth
    for i in range(CHUNKS):
        loads[i].wait()
        lax.fori_loop(i * per_chunk, (i + 1) * per_chunk, first_peaks, 0)

    part_c1[...] = tile_peaks(term_b[...], order_c, sorted_c, last_c, True)
    pl.semaphore_wait(barrier, n_row + n_col - 2)
    send_c1 = scatter(1, "row", part_c1, recv_c1)
    send_c1.start()
    part_r1[...] = tile_peaks(term_a[...], order_r, sorted_r, last_r, True)
    send_r1 = scatter(0, "col", part_r1, recv_r1)
    send_r1.start()

    for copy in local[2:]:
        copy.wait()
    pick_h[...] = dot(gather_r[...], dual_full[...].astype(BF16)).astype(BF16)
    products(pick_h, term_a, kv)
    part_g1[...] = select_dot(spread_c[...], term_a[...])

    row_scale = 1.0 / jnp.sqrt(collect(send_r1, part_r1, row_at, recv_r1, jnp.maximum) + SMALL_EPS)
    full_r1[row_at, :] = row_scale
    share_r1 = spread_out(2, "col", full_r1.at[row_at], full_r1.at[row_at])
    share_r1.start()
    col_scale = 1.0 / jnp.sqrt(collect(send_c1, part_c1, col_at, recv_c1, jnp.maximum) + SMALL_EPS)
    full_c1[col_at, :] = col_scale
    share_c1 = spread_out(3, "row", full_c1.at[col_at], full_c1.at[col_at])
    share_c1.start()

    share_r1.wait_recv()
    pick_a[...] = select_dot(gather_r[...], full_r1[...])
    share_c1.wait_recv()
    send_g1 = scatter(4, "row", part_g1, recv_g1)
    send_g1.start()
    pick_b[...] = select_dot(gather_c[...], full_c1[...])

    wide_at = (2 * eighth, eighth * LANES)
    spreader = one_hot(iota(wide_at, 0) % eighth == iota(wide_at, 1) // LANES)

    def second_peaks(g, carry):
        base = pl.multiple_of(g * eighth, eighth)
        place = iota((eighth, LANES), 0)
        by_row = jnp.zeros((eighth, LANES), F32)
        by_col = jnp.zeros((eighth, LANES), F32)
        row_part = pick_a[pl.ds(base, eighth), :]
        col_part = pick_b[pl.ds(base, eighth), :]
        high = row_part.astype(BF16).astype(F32)
        high2 = col_part.astype(BF16).astype(F32)
        col_down = jnp.concatenate([high2, col_part - high2], axis=0).T.astype(BF16)
        row_down = jnp.concatenate([high, row_part - high], axis=0).T.astype(BF16)
        for b in range(eighth):
            if b % 4 < 2:
                if b % 2 == 0:
                    wide2 = dot(col_down, spreader[:, b * LANES:(b + 2) * LANES])
                size = jnp.abs(kvt[base + b].astype(F32)) * wide2[:, (b % 2) * LANES:(b % 2 + 1) * LANES]
                across_peak = jnp.max(size, axis=0, keepdims=True)
            else:
                size = jnp.abs(kv[base + b].astype(F32)) * col_part[b:b + 1]
                across_peak = on_diagonal(jnp.max(size, axis=1, keepdims=True))
            if b % 2 == 0:
                wide = dot(row_down, spreader[:, b * LANES:(b + 2) * LANES])
            size = jnp.abs(kv[base + b].astype(F32)) * wide[:, (b % 2) * LANES:(b % 2 + 1) * LANES]
            down_peak = jnp.max(size, axis=0, keepdims=True)
            by_row = jnp.where(place == b, across_peak, by_row)
            by_col = jnp.where(place == b, down_peak, by_col)
        term_a[pl.ds(base, eighth), :] = by_row * row_part
        term_b[pl.ds(base, eighth), :] = by_col * col_part
        return carry
    most = slots // eighth // 4 * 3
    lax.fori_loop(0, most, second_peaks, 0, unroll=4)
    full_g1[col_at, :] = collect(send_g1, part_g1, col_at, recv_g1, jnp.add)
    share_g1 = spread_out(9, "row", full_g1.at[col_at], full_g1.at[col_at])
    share_g1.start()
    lax.fori_loop(most, slots // eighth, second_peaks, 0, unroll=4)

    part_c2[...] = tile_peaks(term_b[...], order_c, sorted_c, last_c, False)
    send_c2 = scatter(6, "row", part_c2, recv_c2)
    send_c2.start()
    part_r2[...] = tile_peaks(term_a[...], order_r, sorted_r, last_r, False)
    send_r2 = scatter(5, "col", part_r2, recv_r2)
    send_r2.start()
    row_scale = row_scale / jnp.sqrt(collect(send_r2, part_r2, row_at, recv_r2, jnp.maximum) + SMALL_EPS)
    col_scale = col_scale / jnp.sqrt(collect(send_c2, part_c2, col_at, recv_c2, jnp.maximum) + SMALL_EPS)

    full_c2[col_at, :] = col_scale
    share_c2 = spread_out(17, "row", full_c2.at[col_at], full_c2.at[col_at])

    scaled_cost = col_scale * cost_f[col_at, :]
    scaled_demand = row_scale * demand_s[...]

    def squares(x):
        return jnp.sum((x * x).reshape(-1, 8, LANES), axis=0)
    norm_own[0:8, :] = squares(scaled_cost)
    norm_own[8:16, :] = squares(scaled_demand)
    norm_1 = Exchange(7, "col", lambda d, at: (norm_own, norm_x1.at[d]))
    norm_1.start()
    share_c2.start()
    dual_now = dual_s[...] / row_scale
    norm_mid[...] = collect(norm_1, norm_own, slice(None), norm_x1, jnp.add)
    norm_2 = Exchange(8, "row", lambda d, at: (norm_mid, norm_x2.at[d]))
    norm_2.start()

    share_g1.wait_recv()
    share_c2.wait_recv()
    step_rows = 64
    for i in range(0, col_tiles, step_rows):
        at = pl.ds(i, step_rows)
        scale = full_c2[at, :]
        primal_f[at, :] = primal_f[at, :] / scale
        lower_f[at, :] = lower_f[at, :] / scale
        upper_f[at, :] = upper_f[at, :] / scale
        slope_f[at, :] = scale * cost_f[at, :] - scale * full_g1[at, :]
    norms = collect(norm_2, norm_mid, slice(None), norm_x2, jnp.add)
    cost_total = jnp.sum(jnp.sum(norms[0:8], axis=0, keepdims=True), axis=1, keepdims=True)
    demand_total = jnp.sum(jnp.sum(norms[8:16], axis=0, keepdims=True), axis=1, keepdims=True)
    norm_ratio = jnp.sqrt(cost_total + SMALL_EPS) / jnp.sqrt(demand_total + SMALL_EPS)
    primal_step = STEP_SCALE / norm_ratio
    dual_step = STEP_SCALE * norm_ratio

    def project(x, at):
        bound = kind_f[at, :]
        x = jnp.where((bound == 1) | (bound == 3), jnp.maximum(x, lower_f[at, :]), x)
        return jnp.where((bound == 2) | (bound == 3), jnp.minimum(x, upper_f[at, :]), x)

    for i in range(0, col_tiles, step_rows):
        at = pl.ds(i, step_rows)
        primal = primal_f[at, :]
        primal_next = project(primal - primal_step * slope_f[at, :], at)
        full_2[at, :] = (full_c2[at, :] * (2.0 * primal_next - primal)).astype(BF16)
        primal_f[at, :] = primal_next

    half_sh = row_sh // 2
    halves = [slice(h * half_sh, (h + 1) * half_sh) for h in range(2)]
    half_at = [pl.ds(pl.multiple_of(q * row_sh + h * half_sh, 8), half_sh) for h in range(2)]

    def image(numbers, shifted, part, recv):
        pick_h[...] = dot(gather_c[...], shifted).astype(BF16)
        products(pick_h, term_a, kvt)
        sends = []
        for h in range(2):
            starts = range(h * half_sh, row_tiles, row_sh)
            selector = jnp.concatenate([spread_r[i:i + half_sh, :] for i in starts], axis=0)
            sums = select_dot(selector, term_a[...])
            for j, i in enumerate(starts):
                part[i:i + half_sh, :] = sums[j * half_sh:(j + 1) * half_sh]
            sends.append(scatter(numbers[h], "col", part, recv, h, 2))
            sends[h].start()
        return sends

    def next_dual(h, send, part, recv, dual):
        send.wait_recv()
        total = part[half_at[h], :]
        for d in range(1, n_col):
            total = total + recv[d, halves[h], :]
        own = halves[h]
        return jnp.maximum(dual[own] + dual_step * (scaled_demand[own] - row_scale[own] * total), 0.0)

    send_3 = image((10, 18), full_2[...], part_3, recv_3)
    primal = primal_f[col_at, :]

    duals, share_3 = [], []
    for h in range(2):
        duals.append(next_dual(h, send_3[h], part_3, recv_3, dual_now))
        full_3[half_at[h], :] = row_scale[halves[h]] * duals[h]
        share_3.append(spread_out((11, 19)[h], "col", full_3.at[half_at[h]], full_3.at[half_at[h]]))
        share_3[h].start()
    dual_now = jnp.concatenate(duals, axis=0)
    for share in share_3:
        share.wait_recv()
    pick_h[...] = dot(gather_r[...], full_3[...].astype(BF16)).astype(BF16)
    products(pick_h, term_a, kv)
    part_4[...] = select_dot(spread_c[...], term_a[...])
    send_4 = scatter(12, "row", part_4, recv_4)
    send_4.start()
    gradient = col_scale * collect(send_4, part_4, col_at, recv_4, jnp.add)
    primal_next = project(primal - primal_step * (scaled_cost - gradient), col_at)
    full_4[col_at, :] = col_scale * (2.0 * primal_next - primal)
    share_4 = spread_out(13, "row", full_4.at[col_at], full_4.at[col_at])
    share_4.start()
    own_primal[...] = col_scale * primal_next
    keep_p = pltpu.make_async_copy(own_primal, primal_out.at[col_at], local_sem.at[0])
    keep_p.start()
    share_4.wait_recv()
    send_5 = image((15, 20), full_4[...].astype(BF16), part_5, recv_5)
    share_p = spread_out(14, "row", own_primal, primal_out.at[col_at])
    share_p.start()
    share_d, keep_d = [], []
    for h in range(2):
        own_dual[halves[h], :] = row_scale[halves[h]] * next_dual(h, send_5[h], part_5, recv_5, dual_now)
        source, target = own_dual.at[pl.ds(h * half_sh, half_sh)], dual_out.at[half_at[h]]
        share_d.append(spread_out((16, 21)[h], "col", source, target))
        share_d[h].start()
        keep_d.append(pltpu.make_async_copy(source, target, local_sem.at[1 + h]))
        keep_d[h].start()

    for exchange in (
        send_r1, send_c1, share_r1, share_c1, send_g1, share_g1, send_r2, send_c2, share_c2, norm_1, norm_2,
        *send_3, *share_3, send_4, share_4, share_p, *send_5,
    ):
        exchange.wait_send()
    share_p.wait_recv()
    keep_p.wait()
    for h in range(2):
        keep_d[h].wait()
    for share in share_d:
        share.wait_recv()
    for share in share_d:
        share.wait_send()


def keep(primal, dual, primal_out, dual_out, primal_held, dual_held, sems):
    reads, writes = [], []
    for source, held, target in ((primal, primal_held, primal_out), (dual, dual_held, dual_out)):
        half = held.shape[0] // 2
        for start in (0, half):
            at, number = pl.ds(start, half), len(reads)
            reads.append(pltpu.make_async_copy(source.at[at], held.at[at], sems.at[number]))
            writes.append(pltpu.make_async_copy(held.at[at], target.at[at], sems.at[4 + number]))
    for read in reads:
        read.start()
    for read, write in zip(reads, writes):
        read.wait()
        write.start()
    for write in writes:
        write.wait()


def per_device(n_row, n_col, *args):
    values, rows, cols = args[0][0, 0], args[1][0], args[2][0]
    vectors = [a.reshape(-1, LANES) for a in args[3:]]
    slots = values.shape[0]
    col_tiles, row_tiles = vectors[0].shape[0], vectors[1].shape[0]
    row_sh, col_sh = row_tiles // n_col, col_tiles // n_row
    vmem = pltpu.VMEM

    def index_scratch(tiles):
        return [
            vmem((tiles, slots), BF16), vmem((slots, tiles), BF16), vmem((slots, slots), BF16),
            vmem((slots, LANES), F32), vmem((tiles, slots), BF16),
        ]

    row_full, col_full = vmem((row_tiles, LANES), F32), vmem((col_tiles, LANES), F32)
    row_own, col_own = vmem((row_sh, LANES), F32), vmem((col_sh, LANES), F32)
    row_recv, col_recv = vmem((n_col, row_sh, LANES), F32), vmem((n_row, col_sh, LANES), F32)
    term = vmem((slots, LANES), F32)
    most = max(n_row, n_col)
    scratch = [
        vmem(values.shape, BF16), vmem(values.shape, BF16), vmem((1, slots), I32), vmem((1, slots), I32), row_full,
        col_full, col_full, col_full, vmem((col_tiles, LANES), I32), col_full, col_full, row_own, row_own,
        *index_scratch(row_tiles), *index_scratch(col_tiles),
        term, term, term, term, vmem((slots, LANES), BF16),
        row_full, col_full, col_full, row_full, col_full, row_full, col_full, row_full,
        row_recv, col_recv, col_recv, row_recv, col_recv, row_recv, col_recv, row_recv,
        row_full, col_full, col_full, col_full, vmem((col_tiles, LANES), BF16), row_full, col_full, col_own, row_own,
        vmem((16, LANES), F32), vmem((16, LANES), F32),
        vmem((n_col, 16, LANES), F32), vmem((n_row, 16, LANES), F32),
        pltpu.SemaphoreType.DMA((10,)), pltpu.SemaphoreType.DMA((CHUNKS,)),
        pltpu.SemaphoreType.DMA((22, most)), pltpu.SemaphoreType.DMA((22, most)),
    ]
    anywhere = pl.BlockSpec(memory_space=pltpu.HBM)
    primal, dual = pl.pallas_call(
        functools.partial(kernel, n_row, n_col),
        out_shape=(
            jax.ShapeDtypeStruct((col_tiles, LANES), F32),
            jax.ShapeDtypeStruct((row_tiles, LANES), F32),
        ),
        in_specs=[anywhere] * 10,
        out_specs=(anywhere, anywhere),
        scratch_shapes=scratch,
        compiler_params=pltpu.CompilerParams(
            collective_id=0, has_side_effects=True, vmem_limit_bytes=60 * 1024 * 1024
        ),
    )(values, rows, cols, *vectors)
    primal, dual = pl.pallas_call(
        keep,
        out_shape=(
            jax.ShapeDtypeStruct((col_tiles, LANES), F32),
            jax.ShapeDtypeStruct((row_tiles, LANES), F32),
        ),
        in_specs=[anywhere] * 2,
        out_specs=(anywhere, anywhere),
        scratch_shapes=[col_full, row_full, pltpu.SemaphoreType.DMA((8,))],
    )(primal, dual)
    return primal.reshape(-1), dual.reshape(-1)


def solution(mesh):
    grid = P("row", "col", None)
    return jax.shard_map(
        functools.partial(per_device, mesh.shape["row"], mesh.shape["col"]),
        mesh=mesh,
        in_specs=(
            P("row", "col", None, None, None), grid, grid,
            P("col"), P("row"), P("col"), P("col"), P("col"), P("col"), P("row"),
        ),
        out_specs=(P("col"), P("row")),
        check_vma=False,
    )
```
